32 devices in a mesh: ep: 16 (over z, x, core), fs: 2 (over y).
Axes of the slice: x: 2, y: 2, z: 4, core: 2. Of those that a mesh axis runs over, the one named last changes fastest.
Arguments:
- tokens: bfloat16 [2048, 4096], P('ep', 'fs'), may hold values from -6 to 6
- cotangent: bfloat16 [2048, 4096], P('ep', 'fs'), may hold values from -3 to 3
- gate_probs: bfloat16 [2048, 8], P('ep'), may hold values from 0.019897461 to 0.3984375
- expert_ids: int32 [2048, 8], P('ep'), may hold values from 0 to 15, all different within a row; in each aligned block of 128 rows (0 to 127, 128 to 255, ...) at most 72 rows name the same one
- w_gate: bfloat16 [16, 4096, 768], P('ep', 'fs'), may hold values from -0.09375 to 0.09375
- w_up: bfloat16 [16, 4096, 768], P('ep', 'fs'), may hold values from -0.09375 to 0.09375
- w_down: bfloat16 [16, 768, 4096], P('ep', None, 'fs'), may hold values from -0.21875 to 0.21875
Outputs:
- grad_tokens: bfloat16 [2048, 4096], P('ep', 'fs')
- grad_probs: bfloat16 [2048, 8], P('ep')
- grad_w_gate: bfloat16 [16, 4096, 768], P('ep', 'fs')
- grad_w_up: bfloat16 [16, 4096, 768], P('ep', 'fs')
- grad_w_down: bfloat16 [16, 768, 4096], P('ep', None, 'fs')
The draws below stay inside these ranges and needn't reach their ends.
Inputs may be any that keep to these rules, and one draw needn't show every extreme that they name: `expert_ids`: each token names 8 different experts. Among the 128 tokens of one index of ep, no expert is named by more than 72 of them, and in every draw some expert is named by exactly 72.
All inputs are finite; a program needn't handle non-finite values.
Results may differ from the reference program's by a relative error of at most 0.025.
Values may be sent and summed in bfloat16 or wider, within the bound.
A program may use at most 128 MiB of HBM per device.

```python
import math
import jax
import jax.numpy as jnp
import numpy as np
from jax import lax

D = 4096
FF = 768
TOP = 8
TOK_DEV = 128
EXPERTS = 16
TOKENS = 2048
CAP = 72
N_FS = 2


def steps_of(rng, dims, split, low, top_value):
    def one(axis_at, parts):
        steps = jax.random.uniform(jax.random.fold_in(jax.random.fold_in(rng, 6), axis_at), (parts,), jnp.float32, low / len(split), top_value / len(split))
        return jnp.repeat(jnp.exp(steps), dims[axis_at] // parts).reshape((-1,) + (1,) * (len(dims) - axis_at - 1))

    level = one(*split[0])
    for cut in split[1:]:
        level = level * one(*cut)
    return level


def deal_out(own_key, own, number, rows, count, top, limit, lean):
    ranking = jax.random.permutation(own_key, count)
    heavy_load, usual = shares(count, rows * top, limit, lean, True), shares(count, rows * top, limit, lean, False)
    places = jnp.arange(count)

    def named(tallies, rotation):
        used = int((tallies > 0).sum())
        fixed = max(1, used // 4)
        passed = fixed + (places - fixed + rotation * (used - fixed)) % max(1, count - fixed)
        return jnp.zeros((count,), jnp.int32).at[ranking[jnp.where(places < fixed, places, passed)]].set(jnp.asarray(tallies, jnp.int32))

    tallies = jnp.where(number % 4 == 0, named(heavy_load, number // 4), named(usual, number - number // 4 - 1))
    mixed = jax.random.permutation(jax.random.fold_in(own, 3), count)
    donor, receiver = mixed[0:count // 2 * 2:2], mixed[1:count // 2 * 2:2]
    margin = jnp.minimum(tallies[donor] - 1, limit - tallies[receiver]) // 2
    margin = jnp.where((donor == ranking[0]) | (receiver == ranking[0]) | (tallies[receiver] == 0), 0, jnp.maximum(margin, 0))
    passed = jax.random.randint(jax.random.fold_in(own, 4), (count // 2,), 0, 1 << 20) % (margin + 1)
    tallies = tallies.at[donor].add(-passed).at[receiver].add(passed)
    items = jnp.searchsorted(jnp.cumsum(tallies), jnp.arange(rows * top), side="right").astype(jnp.int32)
    table = items.reshape(top, rows).T
    table = table[jax.random.permutation(jax.random.fold_in(own, 1), rows)]
    rotation = jax.random.randint(jax.random.fold_in(own, 2), (rows, 1), 0, top)
    return jnp.take_along_axis(table, (jnp.arange(top)[None, :] + rotation) % top, axis=1)


def shares(number_of, total, bound, skew, full):
    portions = [(1 << 20) // math.isqrt(standing ** skew) + 1 for standing in range(1, number_of + 1)]
    largest = bound if full else min(bound, max(-(-total // number_of), total * portions[0] // sum(portions)))
    least = 1 if total - largest >= number_of - 1 else 0
    given, rest = [largest] + [least] * (number_of - 1), total - largest - least * (number_of - 1)
    while rest > 0:
        movable = [i for i in range(1, number_of) if given[i] < largest] or [i for i in range(1, number_of) if given[i] < bound]
        pool, budget = sum([portions[i] for i in movable]), rest
        for i in movable:
            addition = min(bound - given[i], max(1, budget * portions[i] // pool), rest)
            given[i] = given[i] + addition
            rest = rest - addition
    return np.array(given)


def centred(key, shape, deviation, most, shards=(), kind=jnp.bfloat16):
    level = steps_of(key, shape, shards, -0.22, 0.18) if shards else 1.0
    entries = jax.random.normal(key, shape, jnp.float32) * deviation * level
    return jnp.minimum(jnp.maximum(entries, -most), most).astype(kind)


def setup_inputs(seed: int = 0) -> dict:
    streams_of = jax.random.split(jax.random.key(seed), 8)
    tokens = centred(streams_of[0], (TOKENS, D), 1.0, 6.0, ((0, 16), (1, 2)))
    cotangent = centred(streams_of[1], (TOKENS, D), 0.5, 3.0, ((0, 16), (1, 2)))
    gate_probs = jnp.clip(jnp.exp(math.log(0.3984375) - 2.9969585 * jax.random.uniform(streams_of[2], (TOKENS, TOP), jnp.float32) ** steps_of(streams_of[2], (TOKENS, TOP), ((0, 16),), -0.2, 0.2)), 0.019897461, 0.3984375).astype(jnp.bfloat16)
    expert_ids_keys = jax.random.split(jax.random.fold_in(streams_of[3], 1), TOKENS // TOK_DEV)
    expert_ids_turns = jax.random.permutation(jax.random.fold_in(streams_of[3], 3), TOKENS // TOK_DEV)
    expert_ids = jax.vmap(lambda own, number: deal_out(jax.random.fold_in(streams_of[3], 2), own, number, TOK_DEV, EXPERTS, TOP, CAP, 1))(expert_ids_keys, expert_ids_turns).reshape((TOKENS, TOP))
    w_gate = centred(streams_of[4], (EXPERTS, D, FF), D ** -0.5, 0.09375, ((0, 16), (1, 2)))
    w_up = centred(streams_of[5], (EXPERTS, D, FF), D ** -0.5, 0.09375, ((0, 16), (1, 2)))
    w_down = centred(streams_of[6], (EXPERTS, FF, D), FF ** -0.5, 0.21875, ((0, 16), (2, 2)))
    return {"tokens": tokens, "cotangent": cotangent, "gate_probs": gate_probs, "expert_ids": expert_ids, "w_gate": w_gate, "w_up": w_up, "w_down": w_down}


def build_slots(routing, experts, capacity):
    flat_ids = routing.reshape(-1).astype(jnp.int32)
    choose = (flat_ids[:, None] == jnp.arange(experts, dtype=jnp.int32)[None, :]).astype(jnp.int32)
    earlier = jnp.cumsum(choose, axis=0) - choose
    position = jnp.sum(earlier * choose, axis=1).astype(jnp.int32)
    slot_of = (flat_ids * capacity + position).astype(jnp.int32)
    pair_number = jnp.arange(flat_ids.shape[0], dtype=jnp.int32) + 1
    filled_by = jnp.zeros((experts * capacity,), jnp.int32).at[slot_of].set(pair_number)
    return slot_of, filled_by


def blocked_sum(product_blocks):
    rounded = lax.optimization_barrier(product_blocks.astype(jnp.bfloat16))
    return jnp.sum(rounded.astype(jnp.float32), axis=1)


def reference(tokens, cotangent, gate_probs, expert_ids, w_gate, w_up, w_down):
    sources = TOKENS // TOK_DEV
    width_block = D // N_FS
    slot_count = sources * CAP
    blocks = expert_ids.reshape(sources, TOK_DEV * TOP)
    slot_of, filled_by = jax.vmap(lambda routing: build_slots(routing, EXPERTS, CAP))(blocks)
    per_expert = filled_by.reshape(sources, EXPERTS, CAP).transpose(1, 0, 2).reshape(EXPERTS, slot_count)
    source_row = jnp.repeat(jnp.arange(sources, dtype=jnp.int32), CAP)
    flat_probs = gate_probs.reshape(-1)

    def expert_step(carry, inputs):
        grad_acc, prob_acc = carry
        filled_row, gate_weight, up_weight, down_weight = inputs
        filled = filled_row > 0
        assign = jnp.maximum(filled_row - 1, 0).astype(jnp.int32)
        token_index = (source_row * TOK_DEV + assign // TOP).astype(jnp.int32)
        pair_index = (token_index * TOP + assign % TOP).astype(jnp.int32)
        token_rows = jnp.where(filled[:, None], tokens[token_index], jnp.zeros((), tokens.dtype))
        grad_rows = jnp.where(filled[:, None], cotangent[token_index], jnp.zeros((), cotangent.dtype))
        prob_rows = jnp.where(filled, flat_probs[pair_index], jnp.zeros((), gate_probs.dtype)).astype(jnp.float32)
        token_blocks = token_rows.astype(jnp.float32).reshape(slot_count, N_FS, width_block)
        gate_blocks = jnp.einsum("snf,nfh->snh", token_blocks, gate_weight.astype(jnp.float32).reshape(N_FS, width_block, FF))
        up_blocks = jnp.einsum("snf,nfh->snh", token_blocks, up_weight.astype(jnp.float32).reshape(N_FS, width_block, FF))
        gate_proj = lax.optimization_barrier(blocked_sum(gate_blocks).astype(jnp.bfloat16)).astype(jnp.float32)
        up_proj = lax.optimization_barrier(blocked_sum(up_blocks).astype(jnp.bfloat16)).astype(jnp.float32)
        sigmoid_gate = jax.nn.sigmoid(gate_proj)
        gate_act = gate_proj * sigmoid_gate
        hidden = (gate_act * up_proj).astype(jnp.bfloat16)
        grad_blocks = grad_rows.astype(jnp.float32).reshape(slot_count, N_FS, width_block)
        down_blocks = jnp.einsum("snf,hnf->snh", grad_blocks, down_weight.astype(jnp.float32).reshape(FF, N_FS, width_block))
        raw_grad = blocked_sum(down_blocks)
        grad_prob = jnp.sum(hidden.astype(jnp.float32) * raw_grad, axis=1).astype(jnp.bfloat16)
        scaled = prob_rows[:, None] * raw_grad
        grad_gate = (scaled * up_proj * sigmoid_gate * (1.0 + gate_proj * (1.0 - sigmoid_gate))).astype(jnp.bfloat16)
        grad_up = (scaled * gate_act).astype(jnp.bfloat16)
        weighted = (prob_rows[:, None] * grad_rows.astype(jnp.float32)).astype(jnp.bfloat16)
        new_gate = jnp.dot(token_rows.T, grad_gate, preferred_element_type=jnp.float32).astype(jnp.bfloat16)
        new_up = jnp.dot(token_rows.T, grad_up, preferred_element_type=jnp.float32).astype(jnp.bfloat16)
        new_down = jnp.dot(hidden.T, weighted, preferred_element_type=jnp.float32).astype(jnp.bfloat16)
        grad_part = (jnp.dot(grad_gate, gate_weight.T, preferred_element_type=jnp.float32)
                     + jnp.dot(grad_up, up_weight.T, preferred_element_type=jnp.float32)).astype(jnp.bfloat16)
        target = jnp.where(filled, token_index, TOKENS).astype(jnp.int32)
        grad_acc = grad_acc.at[target].add(grad_part.astype(jnp.float32), mode="drop")
        pair_target = jnp.where(filled, pair_index, TOKENS * TOP).astype(jnp.int32)
        prob_acc = prob_acc.at[pair_target].add(grad_prob.astype(jnp.float32), mode="drop")
        return (grad_acc, prob_acc), (new_gate, new_up, new_down)

    start_state = (jnp.zeros((TOKENS, D), jnp.float32), jnp.zeros((TOKENS * TOP,), jnp.float32))
    final_state, weight_grads = lax.scan(expert_step, start_state, (per_expert, w_gate, w_up, w_down))
    grad_acc, prob_acc = final_state
    grad_w_gate, grad_w_up, grad_w_down = weight_grads
    return (grad_acc.astype(jnp.bfloat16), prob_acc.reshape(TOKENS, TOP).astype(jnp.bfloat16),
            grad_w_gate, grad_w_up, grad_w_down)
```

```python
import functools

import jax
import jax.numpy as jnp
from jax import lax
from jax.experimental import pallas as pl
from jax.experimental.pallas import tpu as pltpu
from jax.sharding import PartitionSpec as P

BF16, F32 = jnp.bfloat16, jnp.float32
MESH = pl.DeviceIdType.MESH
TOK, COT = 0, 1
ORDER = [
    ("rows", 0, 0),
    ("z", TOK, 1), ("mid", TOK, 3), ("x", TOK, 0),
    ("z", COT, 1), ("mid", COT, 3), ("x", COT, 0),
    ("rows", 1, 0), ("rows", 0, 1),
    ("grads", 0, 0),
    ("z", TOK, 2), ("x", TOK, 1),
    ("grads", 1, 0),
    ("z", COT, 2), ("x", COT, 1),
    ("rows", 1, 1), ("rows", 2, 0),
    ("grads", 0, 1), ("send_x", 0),
    ("z", TOK, 3), ("x", TOK, 2),
    ("grads", 1, 1), ("send_x", 1),
    ("z", COT, 3), ("x", COT, 2),
    ("rows", 2, 1), ("rows", 3, 0),
    ("grads", 2, 0),
    ("x", TOK, 3),
    ("send_z", 0), ("send_z", 1),
    ("grads", 2, 1), ("send_x", 2),
    ("x", COT, 3), ("rows", 3, 1),
    ("send_z", 2),
    ("grads", 3, 0),
    ("grads", 3, 1), ("send_x", 3),
    ("weights", 0, 6),
    ("send_z", 3),
    ("weights", 6, 11),
    ("total",),
]


def tile_of(size, most):
    while size % most:
        most //= 2
    return most


def expert_kernel(
    cap, table, tok, cot, w_gate, w_up, w_down,
    out_tok, out_prob, out_gate, out_up, out_down,
    xs, cs, w_in, w_dn, rows, weighted, grow, part, summed, c_recv, x_recv, z_recv,
    pick, pick_p, prob, gp_col, meta, gp_send, gp_recv, p_rows, stage,
    load_sem, zs_sem, zr_sem, xs_sem, xr_sem, cs_sem, cr_sem, ys_sem, yr_sem,
    bcs_sem, bcr_sem, bxs_sem, bxr_sem, bzs_sem, bzr_sem,
    ms_sem, mr_sem, gs_sem, gr_sem, out_sem,
):
    toks, width = tok.shape
    hid = w_gate.shape[1]
    m = 2 * cap
    ep, fs = lax.axis_index("ep"), lax.axis_index("fs")
    z, x, c = ep // 4, (ep // 2) % 2, ep % 2
    z_of = (z, z + 1 - 2 * (z % 2), (z + 2) % 4, 3 - z)
    x_of, c_of = (x, 1 - x), (c, 1 - c)
    is_mid = jnp.logical_or(z == 1, z == 2)
    is_end = jnp.logical_not(is_mid)
    full = (xs, cs)

    def peer(i, dx, dc):
        return ((z_of[i] * 2 + x_of[dx]) * 2 + c_of[dc], fs)

    y_peer = (ep, 1 - fs)
    peers = [(k // 4, (k // 2) % 2, k % 2) for k in range(16)]
    pending = []

    def remote(src, dst, ssem, rsem, dev):
        return pltpu.make_async_remote_copy(
            src_ref=src, dst_ref=dst, send_sem=ssem, recv_sem=rsem,
            device_id=dev, device_id_type=MESH,
        )

    def send(src, dst, ssem, rsem, dev, when=None):
        copy = remote(src, dst, ssem, rsem, dev)
        pending.append((copy, when))
        if when is None:
            copy.start()
        else:
            pl.when(when)(copy.start)

    def arrived(dst, ssem, rsem):
        remote(dst, dst, ssem, rsem, y_peer).wait_recv()

    def block(a, q):
        return full[a].at[q, pl.ds(0, toks)]

    def other(a, q):
        return full[a].at[q, pl.ds(toks, toks)]

    loads = [
        pltpu.make_async_copy(tok, block(TOK, 0), load_sem.at[0]),
        pltpu.make_async_copy(cot, block(COT, 0), load_sem.at[1]),
        pltpu.make_async_copy(w_gate, w_in.at[:, pl.ds(0, hid)], load_sem.at[2]),
        pltpu.make_async_copy(w_up, w_in.at[:, pl.ds(hid, hid)], load_sem.at[3]),
        pltpu.make_async_copy(w_down, w_dn, load_sem.at[4]),
    ]
    for load in loads:
        load.start()
    barrier = pltpu.get_barrier_semaphore()
    for k in range(1, 16):
        pl.semaphore_signal(barrier, inc=1, device_id=peer(*peers[k]), device_id_type=MESH)
    pl.semaphore_signal(barrier, inc=1, device_id=y_peer, device_id_type=MESH)
    pl.semaphore_wait(barrier, 16)

    def send_core(a, q):
        send(block(a, q), other(a, q), cs_sem.at[a, q], cr_sem.at[a, q], peer(0, 0, 1))

    def send_x(a, i):
        send(block(a, 2 * i), block(a, 2 * i + 1), xs_sem.at[a, i], xr_sem.at[a, i],
             peer(0, 1, 0))

    def send_z(a, i, to, lands, n, when=None):
        send(block(a, 2 * i), block(a, 2 * lands), zs_sem.at[a, n], zr_sem.at[a, lands - 1],
             peer(to, 0, 0), when)

    for k in range(1, 16):
        send(table, meta.at[k], ms_sem.at[k], mr_sem.at[k], peer(*peers[k]))
    for a in (TOK, COT):
        loads[a].wait()
        send_core(a, 0)
        send_z(a, 0, 1, 1, 0)
        send_x(a, 0)
        send_z(a, 0, 3, 3, 1, is_mid)

    expert_row = lax.broadcasted_iota(jnp.int32, (16, toks), 0) == ep
    for k in range(16):
        if k:
            arrived(meta.at[k], ms_sem.at[k], mr_sem.at[k])
        named = (table[...] if k == 0 else meta[k]).astype(F32)
        p_rows[k:k + 1, :] = jnp.sum(jnp.where(expert_row, named, 0.0), axis=0, keepdims=True)
    chosen = p_rows[...] > 0.0
    before = (
        lax.broadcasted_iota(jnp.int32, (toks, toks), 0)
        < lax.broadcasted_iota(jnp.int32, (toks, toks), 1)
    )
    place = jnp.dot(
        jnp.where(chosen, 1.0, 0.0).astype(BF16), jnp.where(before, 1.0, 0.0).astype(BF16),
        preferred_element_type=F32,
    )
    odd = lax.broadcasted_iota(jnp.int32, (16, toks), 0) % 2
    place = jnp.where(chosen, place + (odd * cap).astype(F32), -1.0)
    slot_no = lax.broadcasted_iota(jnp.int32, (m, toks), 0).astype(F32)
    for q in range(8):
        total_p = jnp.zeros((m, 1), F32)
        for h in range(2):
            k = 2 * q + h
            lanes = slice(h * toks, (h + 1) * toks)
            hit = slot_no == place[k:k + 1, :]
            value = jnp.where(hit, p_rows[k:k + 1, :], 0.0)
            pick[q, :, lanes] = jnp.where(hit, 1.0, 0.0).astype(BF16)
            pick_p[q, :, lanes] = value.astype(BF16)
            total_p = total_p + jnp.sum(value, axis=1, keepdims=True)
        prob[q] = jnp.broadcast_to(total_p, (m, 128))
    loads[2].wait()
    loads[3].wait()
    loads[4].wait()

    across_last = (((1,), (1,)), ((), ()))
    across_first = (((0,), (0,)), ((), ()))
    t_w, t_h = tile_of(width, 512), tile_of(hid, 256)
    t_d = tile_of(width, 256)

    def cols(n, t):
        return pl.ds(pl.multiple_of(n * t, t), t)

    def do_rows(i, dx):
        q = 2 * i + dx
        mine = pl.ds(q * m, m)
        arrived(other(TOK, q), cs_sem.at[TOK, q], cr_sem.at[TOK, q])

        @pl.loop(0, width // t_w)
        def _(n):
            rows[mine, cols(n, t_w)] = jnp.dot(
                pick[q], xs[q, :, cols(n, t_w)], preferred_element_type=F32
            ).astype(BF16)

        @pl.loop(0, 2 * hid // t_h)
        def _(n):
            part[mine, cols(n, t_h)] = jnp.dot(
                rows[mine, :], w_in[:, cols(n, t_h)], preferred_element_type=F32
            ).astype(BF16)

        arrived(other(COT, q), cs_sem.at[COT, q], cr_sem.at[COT, q])

        @pl.loop(0, width // t_w)
        def _(n):
            block_c = cs[q, :, cols(n, t_w)]
            grow[:, cols(n, t_w)] = jnp.dot(
                pick[q], block_c, preferred_element_type=F32
            ).astype(BF16)
            weighted[mine, cols(n, t_w)] = jnp.dot(
                pick_p[q], block_c, preferred_element_type=F32
            ).astype(BF16)

        @pl.loop(0, hid // t_h)
        def _(n):
            part[mine, pl.ds(pl.multiple_of(2 * hid + n * t_h, t_h), t_h)] = lax.dot_general(
                grow[...], w_dn[cols(n, t_h), :], across_last, preferred_element_type=F32
            ).astype(BF16)

        send(part.at[mine], summed.at[mine], ys_sem.at[q], yr_sem.at[q], y_peer)

    def do_grads(i, dx):
        q = 2 * i + dx
        mine = pl.ds(q * m, m)
        arrived(summed.at[mine], ys_sem.at[q], yr_sem.at[q])

        @pl.loop(0, m // 16)
        def _(r):
            at = pl.ds(pl.multiple_of(q * m + r * 16, 16), 16)
            here = pl.ds(pl.multiple_of(r * 16, 16), 16)

            def both(n):
                lanes = slice(n * hid, (n + 1) * hid)
                return part[at, lanes].astype(F32) + summed[at, lanes].astype(F32)

            gate = both(0).astype(BF16).astype(F32)
            up = both(1).astype(BF16).astype(F32)
            raw = both(2)
            sig = jax.nn.sigmoid(gate)
            act = gate * sig
            hidden = (act * up).astype(BF16)
            scaled = prob[q, here, :][:, :1] * raw
            grad_gate = scaled * up * sig * (1.0 + gate * (1.0 - sig))
            summed[at, 0:hid] = hidden
            summed[at, hid:2 * hid] = grad_gate.astype(BF16)
            summed[at, 2 * hid:3 * hid] = (scaled * act).astype(BF16)
            grad_p = jnp.sum(hidden.astype(F32) * raw, axis=1, keepdims=True)
            gp_col[here, :] = jnp.broadcast_to(grad_p, (16, 128))

        for h in range(2):
            k = 2 * q + h
            lanes = slice(h * toks, (h + 1) * toks)
            value = jnp.sum(
                jnp.where(pick[q, :, lanes].astype(F32) > 0.0, gp_col[...], 0.0),
                axis=0, keepdims=True,
            )
            tile = jnp.where(expert_row, jnp.broadcast_to(value, (16, toks)), 0.0).astype(BF16)
            if k == 0:
                gp_recv[0] = tile
            else:
                gp_send[k] = tile
                send(gp_send.at[k], gp_recv.at[k], gs_sem.at[k], gr_sem.at[k], peer(*peers[k]))

        @pl.loop(0, width // t_d)
        def _(n):
            back = lax.dot_general(
                summed[mine, hid:3 * hid], w_in[cols(n, t_d), :], across_last,
                preferred_element_type=F32,
            ).astype(BF16)
            dense = lax.dot_general(
                pick[q], back, across_first, preferred_element_type=F32
            ).astype(BF16)
            cs[q, toks:2 * toks, cols(n, t_d)] = dense[:toks]
            xs[q, toks:2 * toks, cols(n, t_d)] = dense[toks:]

        send(other(TOK, q), c_recv.at[q], bcs_sem.at[q], bcr_sem.at[q], peer(0, 0, 1))

    def add_into(q, terms, out=None):
        @pl.loop(0, toks // 16)
        def _(r):
            here = pl.ds(pl.multiple_of(r * 16, 16), 16)
            mine = pl.ds(pl.multiple_of(toks + r * 16, 16), 16)
            total = cs[q, mine, :].astype(F32)
            for ref, n in terms:
                total = total + ref[n, here, :].astype(F32)
            if out is None:
                cs[q, mine, :] = total.astype(BF16)
            else:
                out[here, :] = total.astype(BF16)

    def core_arrived(q):
        arrived(c_recv.at[q], bcs_sem.at[q], bcr_sem.at[q])

    def copy_out(u, fn):
        if u < 8:
            t = width // 8
            fn(pltpu.make_async_copy(
                stage.at[u % 2, pl.ds(0, t), pl.ds(0, hid)],
                out_gate.at[pl.ds(u * t, t)], out_sem.at[u % 2, 0]))
            fn(pltpu.make_async_copy(
                stage.at[u % 2, pl.ds(0, t), pl.ds(hid, hid)],
                out_up.at[pl.ds(u * t, t)], out_sem.at[u % 2, 1]))
        else:
            t = hid // 3
            fn(pltpu.make_async_copy(
                stage.at[u % 2, pl.ds(0, t), pl.ds(0, width)],
                out_down.at[pl.ds((u - 8) * t, t)], out_sem.at[u % 2, 0]))

    def do_weights(first, last):
        for u in range(first, last):
            if u >= 2:
                copy_out(u - 2, lambda copy: copy.wait())
            if u < 8:
                t = width // 8
                lhs, l_at, rhs, r_at, count = rows, u * t, summed, hid, 2 * hid
            else:
                t = hid // 3
                lhs, l_at, rhs, r_at, count = summed, (u - 8) * t, weighted, 0, width
            t_n = tile_of(count, 512)

            @pl.loop(0, count // t_n)
            def _(n):
                stage[u % 2, 0:t, cols(n, t_n)] = lax.dot_general(
                    lhs[:, l_at:l_at + t],
                    rhs[:, pl.ds(pl.multiple_of(r_at + n * t_n, 128), t_n)],
                    across_first, preferred_element_type=F32,
                ).astype(BF16)

            copy_out(u, lambda copy: copy.start())

    for task, *which in ORDER:
        if task == "rows":
            do_rows(*which)
        elif task == "grads":
            do_grads(*which)
        elif task == "z":
            a, i = which
            q = 2 * i
            wait = functools.partial(
                arrived, block(a, q), zs_sem.at[a, 0], zr_sem.at[a, i - 1]
            )
            if i == 3:
                pl.when(is_end)(wait)
            else:
                wait()
            if i == 1:
                send_z(a, 1, 3, 2, 2, is_mid)
            if i == 2:
                send_z(a, 2, 1, 3, 3, is_mid)
            send_x(a, i)
            send_core(a, q)
        elif task == "mid":
            a, i = which
            pl.when(is_mid)(
                functools.partial(arrived, block(a, 6), zs_sem.at[a, 0], zr_sem.at[a, 2])
            )
            send_z(a, 3, 1, 2, 4, is_mid)
        elif task == "x":
            a, i = which
            arrived(block(a, 2 * i + 1), xs_sem.at[a, i], xr_sem.at[a, i])
            send_core(a, 2 * i + 1)
        elif task == "send_x":
            (i,) = which
            q = 2 * i + 1
            core_arrived(q)
            add_into(q, [(c_recv, q)])
            send(other(COT, q), x_recv.at[i], bxs_sem.at[i], bxr_sem.at[i], peer(0, 1, 0))
        elif task == "send_z":
            (i,) = which
            core_arrived(2 * i)
            arrived(x_recv.at[i], bxs_sem.at[i], bxr_sem.at[i])
            add_into(2 * i, [(c_recv, 2 * i), (x_recv, i)])
            if i:
                send(other(COT, 2 * i), z_recv.at[i - 1], bzs_sem.at[i - 1],
                     bzr_sem.at[i - 1], peer(i, 0, 0))
        elif task == "weights":
            do_weights(*which)
        elif task == "total":
            for n in range(3):
                arrived(z_recv.at[n], bzs_sem.at[n], bzr_sem.at[n])
            add_into(0, [(z_recv, 0), (z_recv, 1), (z_recv, 2)], out_tok)
            for k in range(1, 16):
                arrived(gp_recv.at[k], gs_sem.at[k], gr_sem.at[k])
            total = gp_recv[0].astype(F32)
            for k in range(1, 16):
                total = total + gp_recv[k].astype(F32)
            out_prob[...] = total
    copy_out(9, lambda copy: copy.wait())
    copy_out(10, lambda copy: copy.wait())
    for copy, when in pending:
        if when is None:
            copy.wait_send()
        else:
            pl.when(when)(copy.wait_send)


def per_device_fused(tokens, cotangent, gate_probs, expert_ids, w_gate, w_up, w_down):
    toks, top_count = expert_ids.shape
    width, hid = tokens.shape[1], w_gate.shape[2]
    cap = slot_capacity(toks, top_count, 16)
    m, slots = 2 * cap, 16 * cap
    numbers = jnp.arange(16, dtype=jnp.int32)
    named = expert_ids[None, :, :] == numbers[:, None, None]
    table = jnp.sum(jnp.where(named, gate_probs[None].astype(F32), 0.0), axis=2).astype(BF16)
    anywhere = pl.BlockSpec(memory_space=pl.ANY)
    vmem = pl.BlockSpec(memory_space=pltpu.VMEM)
    dma = pltpu.SemaphoreType.DMA
    stage_rows, stage_cols = max(width // 8, hid // 3), max(2 * hid, width)
    grad_tokens, grad_table, new_gate, new_up, new_down = pl.pallas_call(
        functools.partial(expert_kernel, cap),
        out_shape=(
            jax.ShapeDtypeStruct((toks, width), BF16),
            jax.ShapeDtypeStruct((16, toks), F32),
            jax.ShapeDtypeStruct((width, hid), BF16),
            jax.ShapeDtypeStruct((width, hid), BF16),
            jax.ShapeDtypeStruct((hid, width), BF16),
        ),
        in_specs=[vmem] + [anywhere] * 5,
        out_specs=(vmem, vmem, anywhere, anywhere, anywhere),
        scratch_shapes=[
            pltpu.VMEM((8, 2 * toks, width), BF16),
            pltpu.VMEM((8, 2 * toks, width), BF16),
            pltpu.VMEM((width, 2 * hid), BF16),
            pltpu.VMEM((hid, width), BF16),
            pltpu.VMEM((slots, width), BF16),
            pltpu.VMEM((slots, width), BF16),
            pltpu.VMEM((m, width), BF16),
            pltpu.VMEM((slots, 3 * hid), BF16),
            pltpu.VMEM((slots, 3 * hid), BF16),
            pltpu.VMEM((8, toks, width), BF16),
            pltpu.VMEM((4, toks, width), BF16),
            pltpu.VMEM((3, toks, width), BF16),
            pltpu.VMEM((8, m, 2 * toks), BF16),
            pltpu.VMEM((8, m, 2 * toks), BF16),
            pltpu.VMEM((8, m, 128), F32),
            pltpu.VMEM((m, 128), F32),
            pltpu.VMEM((16, 16, toks), BF16),
            pltpu.VMEM((16, 16, toks), BF16),
            pltpu.VMEM((16, 16, toks), BF16),
            pltpu.VMEM((16, toks), F32),
            pltpu.VMEM((2, stage_rows, stage_cols), BF16),
            dma((5,)), dma((2, 5)), dma((2, 3)), dma((2, 4)), dma((2, 4)),
            dma((2, 8)), dma((2, 8)), dma((8,)), dma((8,)),
            dma((8,)), dma((8,)), dma((4,)), dma((4,)), dma((3,)), dma((3,)),
            dma((16,)), dma((16,)), dma((16,)), dma((16,)), dma((2, 2)),
        ],
        compiler_params=pltpu.CompilerParams(
            collective_id=0, has_side_effects=True, vmem_limit_bytes=VMEM_BYTES
        ),
        name="expert_layer",
    )(table, tokens, cotangent, w_gate[0], w_up[0], w_down[0])
    grad_probs = jnp.sum(
        jnp.where(named, grad_table[:, :, None], 0.0), axis=0
    ).astype(BF16)
    return (grad_tokens, grad_probs, new_gate[None], new_up[None], new_down[None])


VMEM_BYTES = 62 * 1024 * 1024


def build_slots(routing, experts, capacity):
    flat_ids = routing.reshape(-1)
    choose = (flat_ids[:, None] == jnp.arange(experts, dtype=jnp.int32)[None, :]).astype(jnp.int32)
    count = flat_ids.shape[0]
    below = jnp.tril(jnp.ones((count, count), jnp.bfloat16), -1)
    earlier = jnp.dot(
        below, choose.astype(jnp.bfloat16), preferred_element_type=jnp.float32
    ).astype(jnp.int32)
    position = jnp.sum(earlier * choose, axis=1)
    slot_of = flat_ids * capacity + position
    pair_number = jnp.arange(flat_ids.shape[0], dtype=jnp.int32) + 1
    filled_by = jnp.zeros((experts * capacity,), jnp.int32).at[slot_of].set(pair_number)
    return (slot_of, filled_by)


def activate(gate_up, hidden_units):
    gate_proj = gate_up[:, :hidden_units].astype(jnp.float32)
    up_proj = gate_up[:, hidden_units:].astype(jnp.float32)
    sigmoid_gate = jax.nn.sigmoid(gate_proj)
    gate_act = gate_proj * sigmoid_gate
    return (gate_proj, up_proj, sigmoid_gate, gate_act)


def local_grads(raw_grad, gate_up, prob_rows, hidden_units):
    gate_proj, up_proj, sigmoid_gate, gate_act = activate(gate_up, hidden_units)
    hidden = (gate_act * up_proj).astype(jnp.bfloat16)
    scaled = prob_rows.astype(jnp.float32)[:, None] * raw_grad
    grad_gate = scaled * up_proj * sigmoid_gate * (1.0 + gate_proj * (1.0 - sigmoid_gate))
    grad_up = scaled * gate_act
    grad_gate_up = jnp.concatenate(
        [grad_gate.astype(jnp.bfloat16), grad_up.astype(jnp.bfloat16)], axis=1
    )
    grad_prob = jnp.sum(hidden.astype(jnp.float32) * raw_grad, axis=1).astype(jnp.bfloat16)
    return (grad_gate_up, grad_prob)


def slot_capacity(tok_dev, top_count, experts):
    return (9 * tok_dev * top_count + 8 * experts - 1) // (8 * experts)


def per_device(tokens, cotangent, gate_probs, expert_ids, w_gate, w_up, w_down):
    arrays = (tokens, cotangent, gate_probs, expert_ids, w_gate, w_up, w_down)
    capacity = slot_capacity(expert_ids.shape[0], expert_ids.shape[1], lax.axis_size("ep"))
    if (
        lax.axis_size("fs") == 2
        and lax.axis_size("ep") == 16
        and capacity % 8 == 0
        and expert_ids.shape[0] == 128
    ):
        return per_device_fused(*arrays)
    return per_device_slots(*arrays)


def per_device_slots(tokens, cotangent, gate_probs, expert_ids, w_gate, w_up, w_down):
    tok_dev, top_count = expert_ids.shape
    experts = lax.axis_size("ep")
    shards = lax.axis_size("fs")
    width_dev = tokens.shape[1]
    hidden_units = w_gate.shape[2]
    capacity = slot_capacity(tok_dev, top_count, experts)
    slot_count = experts * capacity
    share_rows = slot_count // shards
    slot_of, filled_by = build_slots(expert_ids, experts, capacity)
    filled = filled_by > 0
    assign = jnp.maximum(filled_by - 1, 0)
    source_token = assign // top_count
    token_send = jnp.where(
        filled[:, None], jnp.take(tokens, source_token, axis=0), jnp.zeros((), tokens.dtype)
    ).reshape(experts, capacity, width_dev)
    grad_send = jnp.where(
        filled[:, None], jnp.take(cotangent, source_token, axis=0), jnp.zeros((), cotangent.dtype)
    ).reshape(experts, capacity, width_dev)
    prob_send = jnp.where(
        filled, jnp.take(gate_probs.reshape(-1), assign, axis=0), jnp.zeros((), gate_probs.dtype)
    ).reshape(experts, capacity)
    token_recv = lax.all_to_all(token_send, "ep", split_axis=0, concat_axis=0, tiled=True)
    token_rows = token_recv.reshape(slot_count, width_dev)
    stacked = jnp.concatenate([w_gate[0], w_up[0]], axis=1)
    down_local = w_down[0]
    section = token_rows
    summed = lax.psum(
        jnp.dot(section, stacked, preferred_element_type=jnp.float32).astype(jnp.bfloat16), "fs"
    )
    gate_up = lax.optimization_barrier(summed)
    gate_proj, up_proj, sigmoid_gate, gate_act = activate(gate_up, hidden_units)
    hidden = (gate_act * up_proj).astype(jnp.bfloat16)
    grad_recv, prob_recv = (
        lax.all_to_all(grad_send, "ep", split_axis=0, concat_axis=0, tiled=True),
        lax.all_to_all(prob_send, "ep", split_axis=0, concat_axis=0, tiled=True),
    )
    grad_rows = grad_recv.reshape(slot_count, width_dev)
    prob_rows = prob_recv.reshape(slot_count)
    weighted = (prob_rows.astype(jnp.float32)[:, None] * grad_rows.astype(jnp.float32)).astype(
        jnp.bfloat16
    )
    across_last = (((1,), (1,)), ((), ()))
    across_first = (((0,), (0,)), ((), ()))
    section = grad_rows
    raw_share = lax.psum_scatter(
        lax.dot_general(
            section, down_local, across_last, preferred_element_type=jnp.float32
        ).astype(jnp.bfloat16),
        "fs",
        scatter_dimension=0,
        tiled=True,
    ).astype(jnp.float32)
    first_row = lax.axis_index("fs") * share_rows
    share_gate_up = lax.dynamic_slice_in_dim(gate_up, first_row, share_rows, 0)
    share_prob_rows = lax.dynamic_slice_in_dim(prob_rows, first_row, share_rows, 0)
    share_grads, share_probs = local_grads(raw_share, share_gate_up, share_prob_rows, hidden_units)
    grad_gate_up, grad_prob = (
        lax.all_gather(share_grads, "fs", axis=0, tiled=True),
        lax.all_gather(share_probs, "fs", axis=0, tiled=True),
    )
    new_down = lax.dot_general(
        hidden, weighted, across_first, preferred_element_type=jnp.float32
    ).astype(jnp.bfloat16)
    joint = lax.dot_general(
        token_rows, grad_gate_up, across_first, preferred_element_type=jnp.float32
    ).astype(jnp.bfloat16)
    new_gate = joint[:, :hidden_units]
    new_up = joint[:, hidden_units:]
    grad_part = lax.dot_general(
        grad_gate_up, stacked, across_last, preferred_element_type=jnp.float32
    ).astype(jnp.bfloat16)
    part_back, prob_back = (
        lax.all_to_all(
            grad_part.reshape(experts, capacity, width_dev),
            "ep",
            split_axis=0,
            concat_axis=0,
            tiled=True,
        ),
        lax.all_to_all(
            grad_prob.reshape(experts, capacity), "ep", split_axis=0, concat_axis=0, tiled=True
        ),
    )
    returned = jnp.take(part_back.reshape(slot_count, width_dev), slot_of, axis=0)
    grad_tokens = jnp.sum(
        returned.reshape(tok_dev, top_count, width_dev).astype(jnp.float32), axis=1
    ).astype(jnp.bfloat16)
    grad_probs = jnp.take(prob_back.reshape(slot_count), slot_of, axis=0).reshape(
        tok_dev, top_count
    )
    return (grad_tokens, grad_probs, new_gate[None], new_up[None], new_down[None])


def solution(mesh):
    return jax.shard_map(
        per_device,
        mesh=mesh,
        in_specs=(
            P("ep", "fs"),
            P("ep", "fs"),
            P("ep", None),
            P("ep", None),
            P("ep", "fs", None),
            P("ep", "fs", None),
            P("ep", None, "fs"),
        ),
        out_specs=(
            P("ep", "fs"),
            P("ep", None),
            P("ep", "fs", None),
            P("ep", "fs", None),
            P("ep", None, "fs"),
        ),
        check_vma=False,
    )
```

```python
import functools

import jax
import jax.numpy as jnp
from jax import lax
from jax.experimental import pallas as pl
from jax.experimental.pallas import tpu as pltpu
from jax.sharding import PartitionSpec as P

BF16, F32 = jnp.bfloat16, jnp.float32
MESH = pl.DeviceIdType.MESH
TOK, COT = 0, 1
TILE_ROWS, TILE_IN, TILE_BACK, TILE_OUT = 1024, 768, 1024, 1024
ORDER = [
    ("rows", 0, 0),
    ("z", TOK, 1), ("mid", TOK, 3), ("x", TOK, 0),
    ("turn",),
    ("z", COT, 1), ("mid", COT, 3), ("x", COT, 0),
    ("rows", 1, 0), ("rows", 0, 1),
    ("grads", 0, 0),
    ("z", TOK, 2), ("x", TOK, 1),
    ("grads", 1, 0),
    ("z", COT, 2), ("x", COT, 1),
    ("rows", 1, 1), ("rows", 2, 0),
    ("grads", 0, 1), ("send_x", 0),
    ("z", TOK, 3), ("x", TOK, 2),
    ("grads", 1, 1), ("send_x", 1),
    ("z", COT, 3), ("x", COT, 2),
    ("rows", 2, 1), ("rows", 3, 0),
    ("grads", 2, 0),
    ("x", TOK, 3),
    ("send_z", 0), ("send_z", 1),
    ("grads", 2, 1), ("send_x", 2),
    ("x", COT, 3), ("rows", 3, 1),
    ("send_z", 2),
    ("grads", 3, 0),
    ("grads", 3, 1), ("send_x", 3),
    ("weights", 0, 6),
    ("send_z", 3),
    ("weights", 6, 11),
    ("total",),
]


def tile_of(size, most):
    while size % most:
        most //= 2
    return most


def expert_kernel(
    cap, table, tok, cot, w_gate, w_up, w_down,
    out_tok, out_prob, out_gate, out_up, out_down,
    xs, cs, w_in, w_back, w_raw, rows, weighted, part, summed, c_recv, x_recv, z_recv,
    pick, pick_p, pick_t, prob, gp_col, meta, gp_send, gp_recv, p_rows,
    load_sem, zs_sem, zr_sem, xs_sem, xr_sem, cs_sem, cr_sem, ys_sem, yr_sem,
    bcs_sem, bcr_sem, bxs_sem, bxr_sem, bzs_sem, bzr_sem,
    ms_sem, mr_sem, gs_sem, gr_sem, out_sem,
):
    toks, width = tok.shape
    hid = w_gate.shape[1]
    m = 2 * cap
    ep, fs = lax.axis_index("ep"), lax.axis_index("fs")
    z, x, c = ep // 4, (ep // 2) % 2, ep % 2
    z_of = (z, z + 1 - 2 * (z % 2), (z + 2) % 4, 3 - z)
    x_of, c_of = (x, 1 - x), (c, 1 - c)
    is_mid = jnp.logical_or(z == 1, z == 2)
    is_end = jnp.logical_not(is_mid)
    full = (xs, cs)

    def peer(i, dx, dc):
        return ((z_of[i] * 2 + x_of[dx]) * 2 + c_of[dc], fs)

    y_peer = (ep, 1 - fs)
    peers = [(k // 4, (k // 2) % 2, k % 2) for k in range(16)]
    pending, y_copies = [], []

    def remote(src, dst, ssem, rsem, dev):
        return pltpu.make_async_remote_copy(
            src_ref=src, dst_ref=dst, send_sem=ssem, recv_sem=rsem,
            device_id=dev, device_id_type=MESH,
        )

    def send(src, dst, ssem, rsem, dev, when=None):
        copy = remote(src, dst, ssem, rsem, dev)
        pending.append((copy, when))
        if when is None:
            copy.start()
        else:
            pl.when(when)(copy.start)

    def arrived(dst, ssem, rsem):
        remote(dst, dst, ssem, rsem, y_peer).wait_recv()

    def block(a, q):
        return full[a].at[q, pl.ds(0, toks)]

    def other(a, q):
        return full[a].at[q, pl.ds(toks, toks)]

    loads = [
        pltpu.make_async_copy(tok, block(TOK, 0), load_sem.at[0]),
        pltpu.make_async_copy(cot, block(COT, 0), load_sem.at[1]),
        pltpu.make_async_copy(w_gate, w_in.at[:, pl.ds(0, hid)], load_sem.at[2]),
        pltpu.make_async_copy(w_up, w_in.at[:, pl.ds(hid, hid)], load_sem.at[3]),
        pltpu.make_async_copy(w_down, part.at[pl.ds(0, hid), pl.ds(0, width)], load_sem.at[4]),
    ]
    for load in loads:
        load.start()
    barrier = pltpu.get_barrier_semaphore()
    for k in range(1, 16):
        pl.semaphore_signal(barrier, inc=1, device_id=peer(*peers[k]), device_id_type=MESH)
    pl.semaphore_signal(barrier, inc=1, device_id=y_peer, device_id_type=MESH)
    pl.semaphore_wait(barrier, 16)

    def send_core(a, q):
        send(block(a, q), other(a, q), cs_sem.at[a, q], cr_sem.at[a, q], peer(0, 0, 1))

    def send_x(a, i):
        send(block(a, 2 * i), block(a, 2 * i + 1), xs_sem.at[a, i], xr_sem.at[a, i],
             peer(0, 1, 0))

    def send_z(a, i, to, lands, n, when=None):
        send(block(a, 2 * i), block(a, 2 * lands), zs_sem.at[a, n], zr_sem.at[a, lands - 1],
             peer(to, 0, 0), when)

    for k in range(1, 16):
        send(table, meta.at[k], ms_sem.at[k], mr_sem.at[k], peer(*peers[k]))
    for a in (TOK, COT):
        loads[a].wait()
        send_core(a, 0)
        send_z(a, 0, 1, 1, 0)
        send_x(a, 0)
        send_z(a, 0, 3, 3, 1, is_mid)

    expert_row = lax.broadcasted_iota(jnp.int32, (16, toks), 0) == ep
    for k in range(16):
        if k:
            arrived(meta.at[k], ms_sem.at[k], mr_sem.at[k])
        named = (table[...] if k == 0 else meta[k]).astype(F32)
        p_rows[k:k + 1, :] = jnp.sum(jnp.where(expert_row, named, 0.0), axis=0, keepdims=True)
    chosen = p_rows[...] > 0.0
    before = (
        lax.broadcasted_iota(jnp.int32, (toks, toks), 0)
        < lax.broadcasted_iota(jnp.int32, (toks, toks), 1)
    )
    place = jnp.dot(
        jnp.where(chosen, 1.0, 0.0).astype(BF16), jnp.where(before, 1.0, 0.0).astype(BF16),
        preferred_element_type=F32,
    )
    odd = lax.broadcasted_iota(jnp.int32, (16, toks), 0) % 2
    place = jnp.where(chosen, place + (odd * cap).astype(F32), -1.0)
    slot_no = lax.broadcasted_iota(jnp.int32, (m, toks), 0).astype(F32)
    for q in range(8):
        total_p = jnp.zeros((m, 1), F32)
        for h in range(2):
            k = 2 * q + h
            lanes = slice(h * toks, (h + 1) * toks)
            hit = slot_no == place[k:k + 1, :]
            value = jnp.where(hit, p_rows[k:k + 1, :], 0.0)
            pick[q, :, lanes] = jnp.where(hit, 1.0, 0.0).astype(BF16)
            pick_p[q, :, lanes] = value.astype(BF16)
            total_p = total_p + jnp.sum(value, axis=1, keepdims=True)
        prob[q] = jnp.broadcast_to(total_p, (m, 128))
    eye = (
        lax.broadcasted_iota(jnp.int32, (toks, toks), 0)
        == lax.broadcasted_iota(jnp.int32, (toks, toks), 1)
    )
    across_last = (((1,), (1,)), ((), ()))
    place_t = lax.dot_general(
        jnp.where(eye, 1.0, 0.0).astype(BF16), place.astype(BF16), across_last,
        preferred_element_type=F32,
    )
    slot_at = lax.broadcasted_iota(jnp.int32, (toks, m), 1).astype(F32)
    for q in range(8):
        for h in range(2):
            k = 2 * q + h
            pick_t[q, h * toks:(h + 1) * toks, :] = jnp.where(
                slot_at == place_t[:, k:k + 1], 1.0, 0.0
            ).astype(BF16)
    t_w, t_h = tile_of(width, TILE_ROWS), tile_of(hid, TILE_IN)
    t_d = tile_of(width, TILE_BACK)
    t_x = tile_of(width, 256)

    def cols(n, t):
        return pl.ds(pl.multiple_of(n * t, t), t)

    loads[4].wait()

    @pl.loop(0, width // t_x)
    def _(n):
        w_raw[cols(n, t_x), :] = part[0:hid, cols(n, t_x)].T

    loads[2].wait()
    loads[3].wait()

    across_first = (((0,), (0,)), ((), ()))

    def turn_weights():
        @pl.loop(0, width // t_x)
        def _(n):
            w_back[:, cols(n, t_x)] = w_in[cols(n, t_x), :].T

    def do_rows(i, dx):
        q = 2 * i + dx
        mine = pl.ds(q * m, m)
        arrived(other(TOK, q), cs_sem.at[TOK, q], cr_sem.at[TOK, q])

        @pl.loop(0, width // t_w)
        def _(n):
            rows[mine, cols(n, t_w)] = jnp.dot(
                pick[q], xs[q, :, cols(n, t_w)], preferred_element_type=F32
            ).astype(BF16)

        @pl.loop(0, 2 * hid // t_h)
        def _(n):
            part[mine, cols(n, t_h)] = jnp.dot(
                rows[mine, :], w_in[:, cols(n, t_h)], preferred_element_type=F32
            ).astype(BF16)

        arrived(other(COT, q), cs_sem.at[COT, q], cr_sem.at[COT, q])

        @pl.loop(0, width // t_w)
        def _(n):
            weighted[mine, cols(n, t_w)] = jnp.dot(
                pick[q], cs[q, :, cols(n, t_w)], preferred_element_type=F32
            ).astype(BF16)

        @pl.loop(0, hid // t_h)
        def _(n):
            part[mine, pl.ds(pl.multiple_of(2 * hid + n * t_h, t_h), t_h)] = jnp.dot(
                weighted[mine, :], w_raw[:, cols(n, t_h)], preferred_element_type=F32
            ).astype(BF16)

        across = remote(part.at[mine], summed.at[mine], ys_sem.at[q], yr_sem.at[q], y_peer)
        across.start()
        y_copies.append(across)

        @pl.loop(0, width // t_w)
        def _(n):
            weighted[mine, cols(n, t_w)] = jnp.dot(
                pick_p[q], cs[q, :, cols(n, t_w)], preferred_element_type=F32
            ).astype(BF16)

    def do_grads(i, dx):
        q = 2 * i + dx
        mine = pl.ds(q * m, m)
        arrived(summed.at[mine], ys_sem.at[q], yr_sem.at[q])

        @pl.loop(0, m // 16)
        def _(r):
            at = pl.ds(pl.multiple_of(q * m + r * 16, 16), 16)
            here = pl.ds(pl.multiple_of(r * 16, 16), 16)

            def both(n):
                lanes = slice(n * hid, (n + 1) * hid)
                return part[at, lanes].astype(F32) + summed[at, lanes].astype(F32)

            gate = both(0).astype(BF16).astype(F32)
            up = both(1).astype(BF16).astype(F32)
            raw = both(2)
            sig = jax.nn.sigmoid(gate)
            act = gate * sig
            hidden = (act * up).astype(BF16)
            scaled = prob[q, here, :][:, :1] * raw
            grad_gate = scaled * up * sig * (1.0 + gate * (1.0 - sig))
            summed[at, 0:hid] = hidden
            summed[at, hid:2 * hid] = grad_gate.astype(BF16)
            summed[at, 2 * hid:3 * hid] = (scaled * act).astype(BF16)
            grad_p = jnp.sum(hidden.astype(F32) * raw, axis=1, keepdims=True)
            gp_col[here, :] = jnp.broadcast_to(grad_p, (16, 128))

        for h in range(2):
            k = 2 * q + h
            lanes = slice(h * toks, (h + 1) * toks)
            value = jnp.sum(
                jnp.where(pick[q, :, lanes].astype(F32) > 0.0, gp_col[...], 0.0),
                axis=0, keepdims=True,
            )
            tile = jnp.where(expert_row, jnp.broadcast_to(value, (16, toks)), 0.0).astype(BF16)
            if k == 0:
                gp_recv[0] = tile
            else:
                gp_send[k] = tile
                send(gp_send.at[k], gp_recv.at[k], gs_sem.at[k], gr_sem.at[k], peer(*peers[k]))

        @pl.loop(0, width // t_d)
        def _(n):
            back = jnp.dot(
                summed[mine, hid:3 * hid], w_back[:, cols(n, t_d)], preferred_element_type=F32
            ).astype(BF16)
            dense = jnp.dot(pick_t[q], back, preferred_element_type=F32).astype(BF16)
            cs[q, toks:2 * toks, cols(n, t_d)] = dense[:toks]
            xs[q, toks:2 * toks, cols(n, t_d)] = dense[toks:]

        send(other(TOK, q), c_recv.at[q], bcs_sem.at[q], bcr_sem.at[q], peer(0, 0, 1))

    def add_into(q, terms, out=None):
        @pl.loop(0, toks // 16)
        def _(r):
            here = pl.ds(pl.multiple_of(r * 16, 16), 16)
            mine = pl.ds(pl.multiple_of(toks + r * 16, 16), 16)
            total = cs[q, mine, :].astype(F32)
            for ref, n in terms:
                total = total + ref[n, here, :].astype(F32)
            if out is None:
                cs[q, mine, :] = total.astype(BF16)
            else:
                out[here, :] = total.astype(BF16)

    def core_arrived(q):
        arrived(c_recv.at[q], bcs_sem.at[q], bcr_sem.at[q])

    def copy_out(u, fn):
        if u < 8:
            t = width // 8
            fn(pltpu.make_async_copy(
                part.at[pl.ds(u % 4 * width // 8, t), pl.ds(0, hid)],
                out_gate.at[pl.ds(u * t, t)], out_sem.at[u % 4, 0]))
            fn(pltpu.make_async_copy(
                part.at[pl.ds(u % 4 * width // 8, t), pl.ds(hid, hid)],
                out_up.at[pl.ds(u * t, t)], out_sem.at[u % 4, 1]))
        else:
            t = hid // 3
            fn(pltpu.make_async_copy(
                part.at[pl.ds(u % 4 * width // 8, t), pl.ds(0, width)],
                out_down.at[pl.ds((u - 8) * t, t)], out_sem.at[u % 4, 0]))

    def do_weights(first, last):
        for u in range(first, last):
            if u >= 4:
                copy_out(u - 4, lambda copy: copy.wait())
            if u < 8:
                t = width // 8
                lhs, l_at, rhs, r_at, count = rows, u * t, summed, hid, 2 * hid
            else:
                t = hid // 3
                lhs, l_at, rhs, r_at, count = summed, (u - 8) * t, weighted, 0, width
            t_n = tile_of(count, TILE_OUT)

            @pl.loop(0, count // t_n)
            def _(n):
                part[u % 4 * width // 8:u % 4 * width // 8 + t, cols(n, t_n)] = lax.dot_general(
                    lhs[:, l_at:l_at + t],
                    rhs[:, pl.ds(pl.multiple_of(r_at + n * t_n, 128), t_n)],
                    across_first, preferred_element_type=F32,
                ).astype(BF16)

            copy_out(u, lambda copy: copy.start())

    for task, *which in ORDER:
        if task == "rows":
            do_rows(*which)
        elif task == "grads":
            do_grads(*which)
        elif task == "z":
            a, i = which
            q = 2 * i
            wait = functools.partial(
                arrived, block(a, q), zs_sem.at[a, 0], zr_sem.at[a, i - 1]
            )
            if i == 3:
                pl.when(is_end)(wait)
            else:
                wait()
            if i == 1:
                send_z(a, 1, 3, 2, 2, is_mid)
            if i == 2:
                send_z(a, 2, 1, 3, 3, is_mid)
            send_x(a, i)
            send_core(a, q)
        elif task == "mid":
            a, i = which
            pl.when(is_mid)(
                functools.partial(arrived, block(a, 6), zs_sem.at[a, 0], zr_sem.at[a, 2])
            )
            send_z(a, 3, 1, 2, 4, is_mid)
        elif task == "x":
            a, i = which
            arrived(block(a, 2 * i + 1), xs_sem.at[a, i], xr_sem.at[a, i])
            send_core(a, 2 * i + 1)
        elif task == "send_x":
            (i,) = which
            q = 2 * i + 1
            core_arrived(q)
            add_into(q, [(c_recv, q)])
            send(other(COT, q), x_recv.at[i], bxs_sem.at[i], bxr_sem.at[i], peer(0, 1, 0))
        elif task == "send_z":
            (i,) = which
            core_arrived(2 * i)
            arrived(x_recv.at[i], bxs_sem.at[i], bxr_sem.at[i])
            add_into(2 * i, [(c_recv, 2 * i), (x_recv, i)])
            if i:
                send(other(COT, 2 * i), z_recv.at[i - 1], bzs_sem.at[i - 1],
                     bzr_sem.at[i - 1], peer(i, 0, 0))
        elif task == "turn":
            turn_weights()
        elif task == "weights":
            while y_copies:
                y_copies.pop().wait_send()
            do_weights(*which)
        elif task == "total":
            for n in range(3):
                arrived(z_recv.at[n], bzs_sem.at[n], bzr_sem.at[n])
            add_into(0, [(z_recv, 0), (z_recv, 1), (z_recv, 2)], out_tok)
            for k in range(1, 16):
                arrived(gp_recv.at[k], gs_sem.at[k], gr_sem.at[k])
            total = gp_recv[0].astype(F32)
            for k in range(1, 16):
                total = total + gp_recv[k].astype(F32)
            out_prob[...] = total
    for u in range(7, 11):
        copy_out(u, lambda copy: copy.wait())
    for copy, when in pending:
        if when is None:
            copy.wait_send()
        else:
            pl.when(when)(copy.wait_send)


def per_device_fused(tokens, cotangent, gate_probs, expert_ids, w_gate, w_up, w_down):
    toks, top_count = expert_ids.shape
    width, hid = tokens.shape[1], w_gate.shape[2]
    cap = slot_capacity(toks, top_count, 16)
    m, slots = 2 * cap, 16 * cap
    numbers = jnp.arange(16, dtype=jnp.int32)
    named = expert_ids[None, :, :] == numbers[:, None, None]
    table = jnp.sum(jnp.where(named, gate_probs[None].astype(F32), 0.0), axis=2).astype(BF16)
    anywhere = pl.BlockSpec(memory_space=pl.ANY)
    vmem = pl.BlockSpec(memory_space=pltpu.VMEM)
    dma = pltpu.SemaphoreType.DMA
    grad_tokens, grad_table, new_gate, new_up, new_down = pl.pallas_call(
        functools.partial(expert_kernel, cap),
        out_shape=(
            jax.ShapeDtypeStruct((toks, width), BF16),
            jax.ShapeDtypeStruct((16, toks), F32),
            jax.ShapeDtypeStruct((width, hid), BF16),
            jax.ShapeDtypeStruct((width, hid), BF16),
            jax.ShapeDtypeStruct((hid, width), BF16),
        ),
        in_specs=[vmem] + [anywhere] * 5,
        out_specs=(vmem, vmem, anywhere, anywhere, anywhere),
        scratch_shapes=[
            pltpu.VMEM((8, 2 * toks, width), BF16),
            pltpu.VMEM((8, 2 * toks, width), BF16),
            pltpu.VMEM((width, 2 * hid), BF16),
            pltpu.VMEM((2 * hid, width), BF16),
            pltpu.VMEM((width, hid), BF16),
            pltpu.VMEM((slots, width), BF16),
            pltpu.VMEM((slots, width), BF16),
            pltpu.VMEM((slots, 3 * hid), BF16),
            pltpu.VMEM((slots, 3 * hid), BF16),
            pltpu.VMEM((8, toks, width), BF16),
            pltpu.VMEM((4, toks, width), BF16),
            pltpu.VMEM((3, toks, width), BF16),
            pltpu.VMEM((8, m, 2 * toks), BF16),
            pltpu.VMEM((8, m, 2 * toks), BF16),
            pltpu.VMEM((8, 2 * toks, m), BF16),
            pltpu.VMEM((8, m, 128), F32),
            pltpu.VMEM((m, 128), F32),
            pltpu.VMEM((16, 16, toks), BF16),
            pltpu.VMEM((16, 16, toks), BF16),
            pltpu.VMEM((16, 16, toks), BF16),
            pltpu.VMEM((16, toks), F32),
            dma((5,)), dma((2, 5)), dma((2, 3)), dma((2, 4)), dma((2, 4)),
            dma((2, 8)), dma((2, 8)), dma((8,)), dma((8,)),
            dma((8,)), dma((8,)), dma((4,)), dma((4,)), dma((3,)), dma((3,)),
            dma((16,)), dma((16,)), dma((16,)), dma((16,)), dma((4, 2)),
        ],
        compiler_params=pltpu.CompilerParams(
            collective_id=0, has_side_effects=True, vmem_limit_bytes=VMEM_BYTES
        ),
        name="expert_layer",
    )(table, tokens, cotangent, w_gate[0], w_up[0], w_down[0])
    grad_probs = jnp.sum(
        jnp.where(named, grad_table[:, :, None], 0.0), axis=0
    ).astype(BF16)
    return (grad_tokens, grad_probs, new_gate[None], new_up[None], new_down[None])


VMEM_BYTES = 62 * 1024 * 1024


def build_slots(routing, experts, capacity):
    flat_ids = routing.reshape(-1)
    choose = (flat_ids[:, None] == jnp.arange(experts, dtype=jnp.int32)[None, :]).astype(jnp.int32)
    count = flat_ids.shape[0]
    below = jnp.tril(jnp.ones((count, count), jnp.bfloat16), -1)
    earlier = jnp.dot(
        below, choose.astype(jnp.bfloat16), preferred_element_type=jnp.float32
    ).astype(jnp.int32)
    position = jnp.sum(earlier * choose, axis=1)
    slot_of = flat_ids * capacity + position
    pair_number = jnp.arange(flat_ids.shape[0], dtype=jnp.int32) + 1
    filled_by = jnp.zeros((experts * capacity,), jnp.int32).at[slot_of].set(pair_number)
    return (slot_of, filled_by)


def activate(gate_up, hidden_units):
    gate_proj = gate_up[:, :hidden_units].astype(jnp.float32)
    up_proj = gate_up[:, hidden_units:].astype(jnp.float32)
    sigmoid_gate = jax.nn.sigmoid(gate_proj)
    gate_act = gate_proj * sigmoid_gate
    return (gate_proj, up_proj, sigmoid_gate, gate_act)


def local_grads(raw_grad, gate_up, prob_rows, hidden_units):
    gate_proj, up_proj, sigmoid_gate, gate_act = activate(gate_up, hidden_units)
    hidden = (gate_act * up_proj).astype(jnp.bfloat16)
    scaled = prob_rows.astype(jnp.float32)[:, None] * raw_grad
    grad_gate = scaled * up_proj * sigmoid_gate * (1.0 + gate_proj * (1.0 - sigmoid_gate))
    grad_up = scaled * gate_act
    grad_gate_up = jnp.concatenate(
        [grad_gate.astype(jnp.bfloat16), grad_up.astype(jnp.bfloat16)], axis=1
    )
    grad_prob = jnp.sum(hidden.astype(jnp.float32) * raw_grad, axis=1).astype(jnp.bfloat16)
    return (grad_gate_up, grad_prob)


def slot_capacity(tok_dev, top_count, experts):
    return (9 * tok_dev * top_count + 8 * experts - 1) // (8 * experts)


def per_device(tokens, cotangent, gate_probs, expert_ids, w_gate, w_up, w_down):
    arrays = (tokens, cotangent, gate_probs, expert_ids, w_gate, w_up, w_down)
    capacity = slot_capacity(expert_ids.shape[0], expert_ids.shape[1], lax.axis_size("ep"))
    if (
        lax.axis_size("fs") == 2
        and lax.axis_size("ep") == 16
        and capacity % 8 == 0
        and expert_ids.shape[0] == 128
    ):
        return per_device_fused(*arrays)
    return per_device_slots(*arrays)


def per_device_slots(tokens, cotangent, gate_probs, expert_ids, w_gate, w_up, w_down):
    tok_dev, top_count = expert_ids.shape
    experts = lax.axis_size("ep")
    shards = lax.axis_size("fs")
    width_dev = tokens.shape[1]
    hidden_units = w_gate.shape[2]
    capacity = slot_capacity(tok_dev, top_count, experts)
    slot_count = experts * capacity
    share_rows = slot_count // shards
    slot_of, filled_by = build_slots(expert_ids, experts, capacity)
    filled = filled_by > 0
    assign = jnp.maximum(filled_by - 1, 0)
    source_token = assign // top_count
    token_send = jnp.where(
        filled[:, None], jnp.take(tokens, source_token, axis=0), jnp.zeros((), tokens.dtype)
    ).reshape(experts, capacity, width_dev)
    grad_send = jnp.where(
        filled[:, None], jnp.take(cotangent, source_token, axis=0), jnp.zeros((), cotangent.dtype)
    ).reshape(experts, capacity, width_dev)
    prob_send = jnp.where(
        filled, jnp.take(gate_probs.reshape(-1), assign, axis=0), jnp.zeros((), gate_probs.dtype)
    ).reshape(experts, capacity)
    token_recv = lax.all_to_all(token_send, "ep", split_axis=0, concat_axis=0, tiled=True)
    token_rows = token_recv.reshape(slot_count, width_dev)
    stacked = jnp.concatenate([w_gate[0], w_up[0]], axis=1)
    down_local = w_down[0]
    section = token_rows
    summed = lax.psum(
        jnp.dot(section, stacked, preferred_element_type=jnp.float32).astype(jnp.bfloat16), "fs"
    )
    gate_up = lax.optimization_barrier(summed)
    gate_proj, up_proj, sigmoid_gate, gate_act = activate(gate_up, hidden_units)
    hidden = (gate_act * up_proj).astype(jnp.bfloat16)
    grad_recv, prob_recv = (
        lax.all_to_all(grad_send, "ep", split_axis=0, concat_axis=0, tiled=True),
        lax.all_to_all(prob_send, "ep", split_axis=0, concat_axis=0, tiled=True),
    )
    grad_rows = grad_recv.reshape(slot_count, width_dev)
    prob_rows = prob_recv.reshape(slot_count)
    weighted = (prob_rows.astype(jnp.float32)[:, None] * grad_rows.astype(jnp.float32)).astype(
        jnp.bfloat16
    )
    across_last = (((1,), (1,)), ((), ()))
    across_first = (((0,), (0,)), ((), ()))
    section = grad_rows
    raw_share = lax.psum_scatter(
        lax.dot_general(
            section, down_local, across_last, preferred_element_type=jnp.float32
        ).astype(jnp.bfloat16),
        "fs",
        scatter_dimension=0,
        tiled=True,
    ).astype(jnp.float32)
    first_row = lax.axis_index("fs") * share_rows
    share_gate_up = lax.dynamic_slice_in_dim(gate_up, first_row, share_rows, 0)
    share_prob_rows = lax.dynamic_slice_in_dim(prob_rows, first_row, share_rows, 0)
    share_grads, share_probs = local_grads(raw_share, share_gate_up, share_prob_rows, hidden_units)
    grad_gate_up, grad_prob = (
        lax.all_gather(share_grads, "fs", axis=0, tiled=True),
        lax.all_gather(share_probs, "fs", axis=0, tiled=True),
    )
    new_down = lax.dot_general(
        hidden, weighted, across_first, preferred_element_type=jnp.float32
    ).astype(jnp.bfloat16)
    joint = lax.dot_general(
        token_rows, grad_gate_up, across_first, preferred_element_type=jnp.float32
    ).astype(jnp.bfloat16)
    new_gate = joint[:, :hidden_units]
    new_up = joint[:, hidden_units:]
    grad_part = lax.dot_general(
        grad_gate_up, stacked, across_last, preferred_element_type=jnp.float32
    ).astype(jnp.bfloat16)
    part_back, prob_back = (
        lax.all_to_all(
            grad_part.reshape(experts, capacity, width_dev),
            "ep",
            split_axis=0,
            concat_axis=0,
            tiled=True,
        ),
        lax.all_to_all(
            grad_prob.reshape(experts, capacity), "ep", split_axis=0, concat_axis=0, tiled=True
        ),
    )
    returned = jnp.take(part_back.reshape(slot_count, width_dev), slot_of, axis=0)
    grad_tokens = jnp.sum(
        returned.reshape(tok_dev, top_count, width_dev).astype(jnp.float32), axis=1
    ).astype(jnp.bfloat16)
    grad_probs = jnp.take(prob_back.reshape(slot_count), slot_of, axis=0).reshape(
        tok_dev, top_count
    )
    return (grad_tokens, grad_probs, new_gate[None], new_up[None], new_down[None])


def solution(mesh):
    return jax.shard_map(
        per_device,
        mesh=mesh,
        in_specs=(
            P("ep", "fs"),
            P("ep", "fs"),
            P("ep", None),
            P("ep", None),
            P("ep", "fs", None),
            P("ep", "fs", None),
            P("ep", None, "fs"),
        ),
        out_specs=(
            P("ep", "fs"),
            P("ep", None),
            P("ep", "fs", None),
            P("ep", "fs", None),
            P("ep", None, "fs"),
        ),
        check_vma=False,
    )
```

```python
import functools

import jax
import jax.numpy as jnp
from jax import lax
from jax.experimental import pallas as pl
from jax.experimental.pallas import tpu as pltpu
from jax.sharding import PartitionSpec as P

BF16, F32 = jnp.bfloat16, jnp.float32
MESH = pl.DeviceIdType.MESH
TOK, COT = 0, 1
TILE_ROWS, TILE_IN, TILE_BACK, TILE_OUT = 1024, 768, 1024, 1024
ORDER = [
    ("rows", TOK, 0, 0), ("across", TOK, 0, 0),
    ("turn",),
    ("z", TOK, 1), ("mid", TOK, 3), ("x", TOK, 0),
    ("rows", TOK, 0, 1), ("across", TOK, 0, 1),
    ("rows", TOK, 1, 0), ("across", TOK, 1, 0),
    ("z", COT, 1), ("mid", COT, 3), ("x", COT, 0),
    ("rows", COT, 1, 0), ("across", COT, 1, 0),
    ("rows", COT, 0, 1), ("rows", COT, 0, 0),
    ("z", TOK, 2), ("x", TOK, 1),
    ("rows", TOK, 1, 1), ("across", TOK, 1, 1),
    ("rows", TOK, 2, 0), ("across", TOK, 2, 0),
    ("grads", 1, 0),
    ("z", COT, 2), ("x", TOK, 2),
    ("rows", TOK, 2, 1), ("across", TOK, 2, 1),
    ("rows", COT, 2, 0), ("across", COT, 2, 0),
    ("z", TOK, 3), ("x", COT, 2),
    ("rows", COT, 2, 1), ("across", COT, 2, 1),
    ("z", COT, 3), ("by_z",), ("x", TOK, 3),
    ("rows", TOK, 3, 1), ("across", TOK, 3, 1),
    ("grads", 2, 0),
    ("x", COT, 3),
    ("rows", COT, 3, 1), ("across", COT, 3, 1),
    ("grads", 2, 1), ("send_x", 2),
    ("rows", TOK, 3, 0), ("across", TOK, 3, 0),
    ("rows", COT, 3, 0), ("across", COT, 3, 0),
    ("x", COT, 1),
    ("rows", COT, 1, 1), ("across", COT, 1, 1),
    ("across", COT, 0, 1), ("across", COT, 0, 0),
    ("send_z", 2),
    ("grads", 3, 1), ("send_x", 3),
    ("grads", 3, 0), ("send_z", 3),
    ("grads", 1, 1), ("send_x", 1),
    ("grads", 0, 1), ("send_x", 0),
    ("grads", 0, 0),
    ("weights", 0, 3),
    ("send_z", 1),
    ("weights", 3, 11),
    ("send_z", 0),
    ("total",),
]


def tile_of(size, most):
    while size % most:
        most //= 2
    return most


def expert_kernel(
    cap, table, tok, cot, w_gate, w_up, w_down,
    out_tok, out_prob, out_gate, out_up, out_down,
    xs, cs, w_in, w_back, w_raw, rows, weighted, part, summed, c_recv, x_recv, z_recv,
    pick, pick_p, pick_t, prob, gp_col, meta, gp_send, gp_recv, p_rows,
    load_sem, zs_sem, zr_sem, xs_sem, xr_sem, cs_sem, cr_sem, ys_sem, yr_sem,
    bcs_sem, bcr_sem, bxs_sem, bxr_sem, bzs_sem, bzr_sem,
    ms_sem, mr_sem, gs_sem, gr_sem, out_sem,
):
    toks, width = tok.shape
    hid = w_gate.shape[1]
    m = 2 * cap
    ep, fs = lax.axis_index("ep"), lax.axis_index("fs")
    z, x, c = ep // 4, (ep // 2) % 2, ep % 2
    z_of = (z, z + 1 - 2 * (z % 2), (z + 2) % 4, 3 - z)
    x_of, c_of = (x, 1 - x), (c, 1 - c)
    is_mid = jnp.logical_or(z == 1, z == 2)
    is_end = jnp.logical_not(is_mid)
    full = (xs, cs)

    def peer(i, dx, dc):
        return ((z_of[i] * 2 + x_of[dx]) * 2 + c_of[dc], fs)

    y_peer = (ep, 1 - fs)
    peers = [(k // 4, (k // 2) % 2, k % 2) for k in range(16)]
    pending, y_copies = [], []

    def remote(src, dst, ssem, rsem, dev):
        return pltpu.make_async_remote_copy(
            src_ref=src, dst_ref=dst, send_sem=ssem, recv_sem=rsem,
            device_id=dev, device_id_type=MESH,
        )

    def send(src, dst, ssem, rsem, dev, when=None):
        copy = remote(src, dst, ssem, rsem, dev)
        pending.append((copy, when))
        if when is None:
            copy.start()
        else:
            pl.when(when)(copy.start)

    def arrived(dst, ssem, rsem):
        remote(dst, dst, ssem, rsem, y_peer).wait_recv()

    def block(a, q):
        return full[a].at[q, pl.ds(0, toks)]

    def other(a, q):
        return full[a].at[q, pl.ds(toks, toks)]

    loads = [
        pltpu.make_async_copy(tok, block(TOK, 0), load_sem.at[0]),
        pltpu.make_async_copy(cot, block(COT, 0), load_sem.at[1]),
        pltpu.make_async_copy(w_gate, w_in.at[:, pl.ds(0, hid)], load_sem.at[2]),
        pltpu.make_async_copy(w_up, w_in.at[:, pl.ds(hid, hid)], load_sem.at[3]),
        pltpu.make_async_copy(w_down, weighted.at[pl.ds(0, hid)], load_sem.at[4]),
    ]
    loads[TOK].start()
    loads[COT].start()
    barrier = pltpu.get_barrier_semaphore()
    for k in range(1, 16):
        pl.semaphore_signal(barrier, inc=1, device_id=peer(*peers[k]), device_id_type=MESH)
    pl.semaphore_signal(barrier, inc=1, device_id=y_peer, device_id_type=MESH)
    pl.semaphore_wait(barrier, 16)

    def send_core(a, q):
        send(block(a, q), other(a, q), cs_sem.at[a, q], cr_sem.at[a, q], peer(0, 0, 1))

    def send_x(a, i):
        send(block(a, 2 * i), block(a, 2 * i + 1), xs_sem.at[a, i], xr_sem.at[a, i],
             peer(0, 1, 0))

    def send_z(a, i, to, lands, n, when=None):
        send(block(a, 2 * i), block(a, 2 * lands), zs_sem.at[a, n], zr_sem.at[a, lands - 1],
             peer(to, 0, 0), when)

    for k in range(1, 16):
        send(table, meta.at[k], ms_sem.at[k], mr_sem.at[k], peer(*peers[k]))
    for a in (TOK, COT):
        loads[a].wait()
        send_core(a, 0)
        send_z(a, 0, 1, 1, 0)
        send_x(a, 0)
        send_z(a, 0, 3, 3, 1, is_mid)
    for load in loads[2:]:
        load.start()

    expert_row = lax.broadcasted_iota(jnp.int32, (16, toks), 0) == ep
    for k in range(16):
        if k:
            arrived(meta.at[k], ms_sem.at[k], mr_sem.at[k])
        named = (table[...] if k == 0 else meta[k]).astype(F32)
        p_rows[k:k + 1, :] = jnp.sum(jnp.where(expert_row, named, 0.0), axis=0, keepdims=True)
    chosen = p_rows[...] > 0.0
    before = (
        lax.broadcasted_iota(jnp.int32, (toks, toks), 0)
        < lax.broadcasted_iota(jnp.int32, (toks, toks), 1)
    )
    place = jnp.dot(
        jnp.where(chosen, 1.0, 0.0).astype(BF16), jnp.where(before, 1.0, 0.0).astype(BF16),
        preferred_element_type=F32,
    )
    odd = lax.broadcasted_iota(jnp.int32, (16, toks), 0) % 2
    place = jnp.where(chosen, place + (odd * cap).astype(F32), -1.0)
    slot_no = lax.broadcasted_iota(jnp.int32, (m, toks), 0).astype(F32)
    for q in range(8):
        total_p = jnp.zeros((m, 1), F32)
        for h in range(2):
            k = 2 * q + h
            lanes = slice(h * toks, (h + 1) * toks)
            hit = slot_no == place[k:k + 1, :]
            value = jnp.where(hit, p_rows[k:k + 1, :], 0.0)
            pick[q, :, lanes] = jnp.where(hit, 1.0, 0.0).astype(BF16)
            pick_p[q, :, lanes] = value.astype(BF16)
            total_p = total_p + jnp.sum(value, axis=1, keepdims=True)
        prob[q] = jnp.broadcast_to(total_p, (m, 128))
    t_w, t_h = tile_of(width, TILE_ROWS), tile_of(hid, TILE_IN)
    t_d = tile_of(width, TILE_BACK)
    t_x = tile_of(width, 256)

    def cols(n, t):
        return pl.ds(pl.multiple_of(n * t, t), t)

    loads[2].wait()
    loads[3].wait()

    across_first = (((0,), (0,)), ((), ()))

    def turn_weights():
        eye = (
            lax.broadcasted_iota(jnp.int32, (toks, toks), 0)
            == lax.broadcasted_iota(jnp.int32, (toks, toks), 1)
        )
        across_last = (((1,), (1,)), ((), ()))
        place_t = lax.dot_general(
            jnp.where(eye, 1.0, 0.0).astype(BF16), place.astype(BF16), across_last,
            preferred_element_type=F32,
        )
        slot_at = lax.broadcasted_iota(jnp.int32, (toks, m), 1).astype(F32)
        for q in range(8):
            for h in range(2):
                k = 2 * q + h
                pick_t[q, h * toks:(h + 1) * toks, :] = jnp.where(
                    slot_at == place_t[:, k:k + 1], 1.0, 0.0
                ).astype(BF16)
        loads[4].wait()

        @pl.loop(0, width // t_x)
        def _(n):
            w_raw[cols(n, t_x), :] = weighted[0:hid, cols(n, t_x)].T

        @pl.loop(0, width // t_x)
        def _(n):
            w_back[:, cols(n, t_x)] = w_in[cols(n, t_x), :].T

    def do_rows(a, i, dx):
        q = 2 * i + dx
        mine = pl.ds(q * m, m)
        arrived(other(a, q), cs_sem.at[a, q], cr_sem.at[a, q])
        to = rows if a == TOK else weighted

        @pl.loop(0, width // t_w)
        def _(n):
            to[mine, cols(n, t_w)] = jnp.dot(
                pick[q], full[a][q, :, cols(n, t_w)], preferred_element_type=F32
            ).astype(BF16)

        if a == TOK:
            @pl.loop(0, 2 * hid // t_h)
            def _(n):
                part[mine, cols(n, t_h)] = jnp.dot(
                    rows[mine, :], w_in[:, cols(n, t_h)], preferred_element_type=F32
                ).astype(BF16)
        else:
            part[mine, 2 * hid:3 * hid] = jnp.dot(
                weighted[mine, :], w_raw[...], preferred_element_type=F32
            ).astype(BF16)

            @pl.loop(0, width // t_w)
            def _(n):
                weighted[mine, cols(n, t_w)] = jnp.dot(
                    pick_p[q], cs[q, :, cols(n, t_w)], preferred_element_type=F32
                ).astype(BF16)

    def across(a, q):
        at = (pl.ds(q * m, m), pl.ds(a * 2 * hid, (2 - a) * hid))
        return remote(
            part.at[at], summed.at[at], ys_sem.at[a, q], yr_sem.at[a, q], y_peer
        )

    def do_grads(i, dx):
        q = 2 * i + dx
        mine = pl.ds(q * m, m)
        across(TOK, q).wait_recv()
        across(COT, q).wait_recv()

        @pl.loop(0, m // 16)
        def _(r):
            at = pl.ds(pl.multiple_of(q * m + r * 16, 16), 16)
            here = pl.ds(pl.multiple_of(r * 16, 16), 16)

            def both(n):
                lanes = slice(n * hid, (n + 1) * hid)
                return part[at, lanes].astype(F32) + summed[at, lanes].astype(F32)

            gate = both(0).astype(BF16).astype(F32)
            up = both(1).astype(BF16).astype(F32)
            raw = both(2)
            sig = jax.nn.sigmoid(gate)
            act = gate * sig
            hidden = (act * up).astype(BF16)
            scaled = prob[q, here, :][:, :1] * raw
            grad_gate = scaled * up * sig * (1.0 + gate * (1.0 - sig))
            summed[at, 0:hid] = hidden
            summed[at, hid:2 * hid] = grad_gate.astype(BF16)
            summed[at, 2 * hid:3 * hid] = (scaled * act).astype(BF16)
            grad_p = jnp.sum(hidden.astype(F32) * raw, axis=1, keepdims=True)
            gp_col[here, :] = jnp.broadcast_to(grad_p, (16, 128))

        for h in range(2):
            k = 2 * q + h
            lanes = slice(h * toks, (h + 1) * toks)
            value = jnp.sum(
                jnp.where(pick[q, :, lanes].astype(F32) > 0.0, gp_col[...], 0.0),
                axis=0, keepdims=True,
            )
            tile = jnp.where(expert_row, jnp.broadcast_to(value, (16, toks)), 0.0).astype(BF16)
            if k == 0:
                gp_recv[0] = tile
            else:
                gp_send[k] = tile
                send(gp_send.at[k], gp_recv.at[k], gs_sem.at[k], gr_sem.at[k], peer(*peers[k]))

        @pl.loop(0, width // t_d)
        def _(n):
            back = jnp.dot(
                summed[mine, hid:3 * hid], w_back[:, cols(n, t_d)], preferred_element_type=F32
            ).astype(BF16)
            dense = jnp.dot(pick_t[q], back, preferred_element_type=F32).astype(BF16)
            cs[q, toks:2 * toks, cols(n, t_d)] = dense[:toks]
            xs[q, toks:2 * toks, cols(n, t_d)] = dense[toks:]

        send(other(TOK, q), c_recv.at[q], bcs_sem.at[q], bcr_sem.at[q], peer(0, 0, 1))

    def add_into(q, terms, out=None):
        @pl.loop(0, toks // 16)
        def _(r):
            here = pl.ds(pl.multiple_of(r * 16, 16), 16)
            mine = pl.ds(pl.multiple_of(toks + r * 16, 16), 16)
            total = cs[q, mine, :].astype(F32)
            for ref, n in terms:
                total = total + ref[n, here, :].astype(F32)
            if out is None:
                cs[q, mine, :] = total.astype(BF16)
            else:
                out[here, :] = total.astype(BF16)

    def core_arrived(q):
        arrived(c_recv.at[q], bcs_sem.at[q], bcr_sem.at[q])

    def copy_out(u, fn):
        if u < 8:
            t = width // 8
            fn(pltpu.make_async_copy(
                part.at[pl.ds(u % 4 * width // 8, t), pl.ds(0, hid)],
                out_gate.at[pl.ds(u * t, t)], out_sem.at[u % 4, 0]))
            fn(pltpu.make_async_copy(
                part.at[pl.ds(u % 4 * width // 8, t), pl.ds(hid, hid)],
                out_up.at[pl.ds(u * t, t)], out_sem.at[u % 4, 1]))
        else:
            t = hid // 3
            fn(pltpu.make_async_copy(
                part.at[pl.ds(u % 4 * width // 8, t), pl.ds(0, width)],
                out_down.at[pl.ds((u - 8) * t, t)], out_sem.at[u % 4, 0]))

    def do_weights(first, last):
        for u in range(first, last):
            if u >= 4:
                copy_out(u - 4, lambda copy: copy.wait())
            if u < 8:
                t = width // 8
                lhs, l_at, rhs, r_at, count = rows, u * t, summed, hid, 2 * hid
            else:
                t = hid // 3
                lhs, l_at, rhs, r_at, count = summed, (u - 8) * t, weighted, 0, width
            t_n = tile_of(count, TILE_OUT)

            @pl.loop(0, count // t_n)
            def _(n):
                part[u % 4 * width // 8:u % 4 * width // 8 + t, cols(n, t_n)] = lax.dot_general(
                    lhs[:, l_at:l_at + t],
                    rhs[:, pl.ds(pl.multiple_of(r_at + n * t_n, 128), t_n)],
                    across_first, preferred_element_type=F32,
                ).astype(BF16)

            copy_out(u, lambda copy: copy.start())

    for task, *which in ORDER:
        if task == "rows":
            do_rows(*which)
        elif task == "across":
            a, i, dx = which
            copy = across(a, 2 * i + dx)
            copy.start()
            y_copies.append(copy)
        elif task == "by_z":
            send(block(COT, 1), block(COT, 3), zs_sem.at[COT, 5], xr_sem.at[COT, 1],
                 peer(1, 0, 0))
        elif task == "grads":
            do_grads(*which)
        elif task == "z":
            a, i = which
            q = 2 * i
            wait = functools.partial(
                arrived, block(a, q), zs_sem.at[a, 0], zr_sem.at[a, i - 1]
            )
            if i == 3:
                pl.when(is_end)(wait)
            else:
                wait()
            if i == 1:
                send_z(a, 1, 3, 2, 2, is_mid)
            if i == 2:
                send_z(a, 2, 1, 3, 3, is_mid)
            if (a, i) != (COT, 1):
                send_x(a, i)
            send_core(a, q)
        elif task == "mid":
            a, i = which
            pl.when(is_mid)(
                functools.partial(arrived, block(a, 6), zs_sem.at[a, 0], zr_sem.at[a, 2])
            )
            send_z(a, 3, 1, 2, 4, is_mid)
        elif task == "x":
            a, i = which
            arrived(block(a, 2 * i + 1), xs_sem.at[a, i], xr_sem.at[a, i])
            send_core(a, 2 * i + 1)
        elif task == "send_x":
            (i,) = which
            q = 2 * i + 1
            core_arrived(q)
            add_into(q, [(c_recv, q)])
            send(other(COT, q), x_recv.at[i], bxs_sem.at[i], bxr_sem.at[i], peer(0, 1, 0))
        elif task == "send_z":
            (i,) = which
            core_arrived(2 * i)
            arrived(x_recv.at[i], bxs_sem.at[i], bxr_sem.at[i])
            add_into(2 * i, [(c_recv, 2 * i), (x_recv, i)])
            if i:
                send(other(COT, 2 * i), z_recv.at[i - 1], bzs_sem.at[i - 1],
                     bzr_sem.at[i - 1], peer(i, 0, 0))
        elif task == "turn":
            turn_weights()
        elif task == "weights":
            while y_copies:
                y_copies.pop().wait_send()
            do_weights(*which)
        elif task == "total":
            for n in range(3):
                arrived(z_recv.at[n], bzs_sem.at[n], bzr_sem.at[n])
            add_into(0, [(z_recv, 0), (z_recv, 1), (z_recv, 2)], out_tok)
            for k in range(1, 16):
                arrived(gp_recv.at[k], gs_sem.at[k], gr_sem.at[k])
            total = gp_recv[0].astype(F32)
            for k in range(1, 16):
                total = total + gp_recv[k].astype(F32)
            out_prob[...] = total
    for u in range(7, 11):
        copy_out(u, lambda copy: copy.wait())
    for copy, when in pending:
        if when is None:
            copy.wait_send()
        else:
            pl.when(when)(copy.wait_send)


def per_device_fused(tokens, cotangent, gate_probs, expert_ids, w_gate, w_up, w_down):
    toks, top_count = expert_ids.shape
    width, hid = tokens.shape[1], w_gate.shape[2]
    cap = slot_capacity(toks, top_count, 16)
    m, slots = 2 * cap, 16 * cap
    numbers = jnp.arange(16, dtype=jnp.int32)
    named = expert_ids[None, :, :] == numbers[:, None, None]
    table = jnp.sum(jnp.where(named, gate_probs[None].astype(F32), 0.0), axis=2).astype(BF16)
    anywhere = pl.BlockSpec(memory_space=pl.ANY)
    vmem = pl.BlockSpec(memory_space=pltpu.VMEM)
    dma = pltpu.SemaphoreType.DMA
    grad_tokens, grad_table, new_gate, new_up, new_down = pl.pallas_call(
        functools.partial(expert_kernel, cap),
        out_shape=(
            jax.ShapeDtypeStruct((toks, width), BF16),
            jax.ShapeDtypeStruct((16, toks), F32),
            jax.ShapeDtypeStruct((width, hid), BF16),
            jax.ShapeDtypeStruct((width, hid), BF16),
            jax.ShapeDtypeStruct((hid, width), BF16),
        ),
        in_specs=[vmem] + [anywhere] * 5,
        out_specs=(vmem, vmem, anywhere, anywhere, anywhere),
        scratch_shapes=[
            pltpu.VMEM((8, 2 * toks, width), BF16),
            pltpu.VMEM((8, 2 * toks, width), BF16),
            pltpu.VMEM((width, 2 * hid), BF16),
            pltpu.VMEM((2 * hid, width), BF16),
            pltpu.VMEM((width, hid), BF16),
            pltpu.VMEM((slots, width), BF16),
            pltpu.VMEM((slots, width), BF16),
            pltpu.VMEM((slots, 3 * hid), BF16),
            pltpu.VMEM((slots, 3 * hid), BF16),
            pltpu.VMEM((8, toks, width), BF16),
            pltpu.VMEM((4, toks, width), BF16),
            pltpu.VMEM((3, toks, width), BF16),
            pltpu.VMEM((8, m, 2 * toks), BF16),
            pltpu.VMEM((8, m, 2 * toks), BF16),
            pltpu.VMEM((8, 2 * toks, m), BF16),
            pltpu.VMEM((8, m, 128), F32),
            pltpu.VMEM((m, 128), F32),
            pltpu.VMEM((16, 16, toks), BF16),
            pltpu.VMEM((16, 16, toks), BF16),
            pltpu.VMEM((16, 16, toks), BF16),
            pltpu.VMEM((16, toks), F32),
            dma((5,)), dma((2, 6)), dma((2, 3)), dma((2, 4)), dma((2, 4)),
            dma((2, 8)), dma((2, 8)), dma((2, 8)), dma((2, 8)),
            dma((8,)), dma((8,)), dma((4,)), dma((4,)), dma((3,)), dma((3,)),
            dma((16,)), dma((16,)), dma((16,)), dma((16,)), dma((4, 2)),
        ],
        compiler_params=pltpu.CompilerParams(
            collective_id=0, has_side_effects=True, vmem_limit_bytes=VMEM_BYTES
        ),
        name="expert_layer",
    )(table, tokens, cotangent, w_gate[0], w_up[0], w_down[0])
    grad_probs = jnp.sum(
        jnp.where(named, grad_table[:, :, None], 0.0), axis=0
    ).astype(BF16)
    return (grad_tokens, grad_probs, new_gate[None], new_up[None], new_down[None])


VMEM_BYTES = 62 * 1024 * 1024


def build_slots(routing, experts, capacity):
    flat_ids = routing.reshape(-1)
    choose = (flat_ids[:, None] == jnp.arange(experts, dtype=jnp.int32)[None, :]).astype(jnp.int32)
    count = flat_ids.shape[0]
    below = jnp.tril(jnp.ones((count, count), jnp.bfloat16), -1)
    earlier = jnp.dot(
        below, choose.astype(jnp.bfloat16), preferred_element_type=jnp.float32
    ).astype(jnp.int32)
    position = jnp.sum(earlier * choose, axis=1)
    slot_of = flat_ids * capacity + position
    pair_number = jnp.arange(flat_ids.shape[0], dtype=jnp.int32) + 1
    filled_by = jnp.zeros((experts * capacity,), jnp.int32).at[slot_of].set(pair_number)
    return (slot_of, filled_by)


def activate(gate_up, hidden_units):
    gate_proj = gate_up[:, :hidden_units].astype(jnp.float32)
    up_proj = gate_up[:, hidden_units:].astype(jnp.float32)
    sigmoid_gate = jax.nn.sigmoid(gate_proj)
    gate_act = gate_proj * sigmoid_gate
    return (gate_proj, up_proj, sigmoid_gate, gate_act)


def local_grads(raw_grad, gate_up, prob_rows, hidden_units):
    gate_proj, up_proj, sigmoid_gate, gate_act = activate(gate_up, hidden_units)
    hidden = (gate_act * up_proj).astype(jnp.bfloat16)
    scaled = prob_rows.astype(jnp.float32)[:, None] * raw_grad
    grad_gate = scaled * up_proj * sigmoid_gate * (1.0 + gate_proj * (1.0 - sigmoid_gate))
    grad_up = scaled * gate_act
    grad_gate_up = jnp.concatenate(
        [grad_gate.astype(jnp.bfloat16), grad_up.astype(jnp.bfloat16)], axis=1
    )
    grad_prob = jnp.sum(hidden.astype(jnp.float32) * raw_grad, axis=1).astype(jnp.bfloat16)
    return (grad_gate_up, grad_prob)


def slot_capacity(tok_dev, top_count, experts):
    return (9 * tok_dev * top_count + 8 * experts - 1) // (8 * experts)


def per_device(tokens, cotangent, gate_probs, expert_ids, w_gate, w_up, w_down):
    arrays = (tokens, cotangent, gate_probs, expert_ids, w_gate, w_up, w_down)
    capacity = slot_capacity(expert_ids.shape[0], expert_ids.shape[1], lax.axis_size("ep"))
    if (
        lax.axis_size("fs") == 2
        and lax.axis_size("ep") == 16
        and capacity % 8 == 0
        and expert_ids.shape[0] == 128
    ):
        return per_device_fused(*arrays)
    return per_device_slots(*arrays)


def per_device_slots(tokens, cotangent, gate_probs, expert_ids, w_gate, w_up, w_down):
    tok_dev, top_count = expert_ids.shape
    experts = lax.axis_size("ep")
    shards = lax.axis_size("fs")
    width_dev = tokens.shape[1]
    hidden_units = w_gate.shape[2]
    capacity = slot_capacity(tok_dev, top_count, experts)
    slot_count = experts * capacity
    share_rows = slot_count // shards
    slot_of, filled_by = build_slots(expert_ids, experts, capacity)
    filled = filled_by > 0
    assign = jnp.maximum(filled_by - 1, 0)
    source_token = assign // top_count
    token_send = jnp.where(
        filled[:, None], jnp.take(tokens, source_token, axis=0), jnp.zeros((), tokens.dtype)
    ).reshape(experts, capacity, width_dev)
    grad_send = jnp.where(
        filled[:, None], jnp.take(cotangent, source_token, axis=0), jnp.zeros((), cotangent.dtype)
    ).reshape(experts, capacity, width_dev)
    prob_send = jnp.where(
        filled, jnp.take(gate_probs.reshape(-1), assign, axis=0), jnp.zeros((), gate_probs.dtype)
    ).reshape(experts, capacity)
    token_recv = lax.all_to_all(token_send, "ep", split_axis=0, concat_axis=0, tiled=True)
    token_rows = token_recv.reshape(slot_count, width_dev)
    stacked = jnp.concatenate([w_gate[0], w_up[0]], axis=1)
    down_local = w_down[0]
    section = token_rows
    summed = lax.psum(
        jnp.dot(section, stacked, preferred_element_type=jnp.float32).astype(jnp.bfloat16), "fs"
    )
    gate_up = lax.optimization_barrier(summed)
    gate_proj, up_proj, sigmoid_gate, gate_act = activate(gate_up, hidden_units)
    hidden = (gate_act * up_proj).astype(jnp.bfloat16)
    grad_recv, prob_recv = (
        lax.all_to_all(grad_send, "ep", split_axis=0, concat_axis=0, tiled=True),
        lax.all_to_all(prob_send, "ep", split_axis=0, concat_axis=0, tiled=True),
    )
    grad_rows = grad_recv.reshape(slot_count, width_dev)
    prob_rows = prob_recv.reshape(slot_count)
    weighted = (prob_rows.astype(jnp.float32)[:, None] * grad_rows.astype(jnp.float32)).astype(
        jnp.bfloat16
    )
    across_last = (((1,), (1,)), ((), ()))
    across_first = (((0,), (0,)), ((), ()))
    section = grad_rows
    raw_share = lax.psum_scatter(
        lax.dot_general(
            section, down_local, across_last, preferred_element_type=jnp.float32
        ).astype(jnp.bfloat16),
        "fs",
        scatter_dimension=0,
        tiled=True,
    ).astype(jnp.float32)
    first_row = lax.axis_index("fs") * share_rows
    share_gate_up = lax.dynamic_slice_in_dim(gate_up, first_row, share_rows, 0)
    share_prob_rows = lax.dynamic_slice_in_dim(prob_rows, first_row, share_rows, 0)
    share_grads, share_probs = local_grads(raw_share, share_gate_up, share_prob_rows, hidden_units)
    grad_gate_up, grad_prob = (
        lax.all_gather(share_grads, "fs", axis=0, tiled=True),
        lax.all_gather(share_probs, "fs", axis=0, tiled=True),
    )
    new_down = lax.dot_general(
        hidden, weighted, across_first, preferred_element_type=jnp.float32
    ).astype(jnp.bfloat16)
    joint = lax.dot_general(
        token_rows, grad_gate_up, across_first, preferred_element_type=jnp.float32
    ).astype(jnp.bfloat16)
    new_gate = joint[:, :hidden_units]
    new_up = joint[:, hidden_units:]
    grad_part = lax.dot_general(
        grad_gate_up, stacked, across_last, preferred_element_type=jnp.float32
    ).astype(jnp.bfloat16)
    part_back, prob_back = (
        lax.all_to_all(
            grad_part.reshape(experts, capacity, width_dev),
            "ep",
            split_axis=0,
            concat_axis=0,
            tiled=True,
        ),
        lax.all_to_all(
            grad_prob.reshape(experts, capacity), "ep", split_axis=0, concat_axis=0, tiled=True
        ),
    )
    returned = jnp.take(part_back.reshape(slot_count, width_dev), slot_of, axis=0)
    grad_tokens = jnp.sum(
        returned.reshape(tok_dev, top_count, width_dev).astype(jnp.float32), axis=1
    ).astype(jnp.bfloat16)
    grad_probs = jnp.take(prob_back.reshape(slot_count), slot_of, axis=0).reshape(
        tok_dev, top_count
    )
    return (grad_tokens, grad_probs, new_gate[None], new_up[None], new_down[None])


def solution(mesh):
    return jax.shard_map(
        per_device,
        mesh=mesh,
        in_specs=(
            P("ep", "fs"),
            P("ep", "fs"),
            P("ep", None),
            P("ep", None),
            P("ep", "fs", None),
            P("ep", "fs", None),
            P("ep", None, "fs"),
        ),
        out_specs=(
            P("ep", "fs"),
            P("ep", None),
            P("ep", "fs", None),
            P("ep", "fs", None),
            P("ep", None, "fs"),
        ),
        check_vma=False,
    )
```

```python
import functools

import jax
import jax.numpy as jnp
from jax import lax
from jax.experimental import pallas as pl
from jax.experimental.pallas import tpu as pltpu
from jax.sharding import PartitionSpec as P

BF16, F32 = jnp.bfloat16, jnp.float32
MESH = pl.DeviceIdType.MESH
TOK, COT = 0, 1
TILE_ROWS, TILE_IN, TILE_BACK, TILE_OUT = 1024, 768, 1024, 1024
ORDER = [
    ("rows", TOK, 0, 0),
    ("across", TOK, 0, 0),
    ("turn",),
    ("z", TOK, 1),
    ("mid", TOK, 3),
    ("x", TOK, 0),
    ("rows", TOK, 0, 1),
    ("across", TOK, 0, 1),
    ("rows", TOK, 1, 0),
    ("across", TOK, 1, 0),
    ("z", COT, 1),
    ("mid", COT, 3),
    ("x", COT, 0),
    ("rows", COT, 1, 0),
    ("across", COT, 1, 0),
    ("rows", COT, 0, 1),
    ("rows", COT, 0, 0),
    ("z", TOK, 2),
    ("x", TOK, 1),
    ("rows", TOK, 1, 1),
    ("across", TOK, 1, 1),
    ("rows", TOK, 2, 0),
    ("across", TOK, 2, 0),
    ("grads", 1, 0),
    ("z", COT, 2),
    ("x", TOK, 2),
    ("rows", TOK, 2, 1),
    ("across", TOK, 2, 1),
    ("rows", COT, 2, 0),
    ("across", COT, 2, 0),
    ("z", TOK, 3),
    ("x", COT, 2),
    ("rows", COT, 2, 1),
    ("across", COT, 2, 1),
    ("z", COT, 3),
    ("by_z",),
    ("x", TOK, 3),
    ("rows", TOK, 3, 1),
    ("across", TOK, 3, 1),
    ("grads", 2, 0),
    ("x", COT, 3),
    ("rows", COT, 3, 1),
    ("across", COT, 3, 1),
    ("grads", 2, 1),
    ("send_x", 2),
    ("rows", TOK, 3, 0),
    ("across", TOK, 3, 0),
    ("rows", COT, 3, 0),
    ("across", COT, 3, 0),
    ("x", COT, 1),
    ("rows", COT, 1, 1),
    ("across", COT, 1, 1),
    ("across", COT, 0, 1),
    ("across", COT, 0, 0),
    ("send_z", 2),
    ("grads", 3, 1),
    ("send_x", 3),
    ("grads", 3, 0),
    ("grads", 1, 1),
    ("send_x", 1),
    ("send_z", 3),
    ("grads", 0, 1),
    ("send_x", 0),
    ("grads", 0, 0),
    ("weights", 0, 3),
    ("send_z", 1),
    ("weights", 3, 11),
    ("send_z", 0),
    ("total",),
]


def tile_of(size, most):
    while size % most:
        most //= 2
    return most


def expert_kernel(
    cap, ids, probs, tok, cot, w_gate, w_up, w_down,
    out_tok, out_prob, out_gate, out_up, out_down,
    table, xs, cs, w_in, w_back, w_raw, rows, weighted, part, summed, c_recv, x_recv, z_recv,
    pick, pick_p, pick_t, place_t, prob, gp_col, meta, gp_send, gp_recv, p_rows,
    load_sem, zs_sem, zr_sem, xs_sem, xr_sem, cs_sem, cr_sem, ys_sem, yr_sem,
    bcs_sem, bcr_sem, bxs_sem, bxr_sem, bzs_sem, bzr_sem,
    ms_sem, mr_sem, gs_sem, gr_sem, out_sem,
):
    toks, width = tok.shape
    hid = w_gate.shape[1]
    m = 2 * cap
    ep, fs = lax.axis_index("ep"), lax.axis_index("fs")
    z, x, c = ep // 4, (ep // 2) % 2, ep % 2
    z_of = (z, z + 1 - 2 * (z % 2), (z + 2) % 4, 3 - z)
    x_of, c_of = (x, 1 - x), (c, 1 - c)
    is_mid = jnp.logical_or(z == 1, z == 2)
    is_end = jnp.logical_not(is_mid)
    full = (xs, cs)

    def peer(i, dx, dc):
        return ((z_of[i] * 2 + x_of[dx]) * 2 + c_of[dc], fs)

    y_peer = (ep, 1 - fs)
    peers = [(k // 4, (k // 2) % 2, k % 2) for k in range(16)]
    pending, y_copies = [], []

    def remote(src, dst, ssem, rsem, dev):
        return pltpu.make_async_remote_copy(
            src_ref=src, dst_ref=dst, send_sem=ssem, recv_sem=rsem,
            device_id=dev, device_id_type=MESH,
        )

    def send(src, dst, ssem, rsem, dev, when=None):
        copy = remote(src, dst, ssem, rsem, dev)
        pending.append((copy, when))
        if when is None:
            copy.start()
        else:
            pl.when(when)(copy.start)

    def arrived(dst, ssem, rsem):
        remote(dst, dst, ssem, rsem, y_peer).wait_recv()

    def block(a, q):
        return full[a].at[q, pl.ds(0, toks)]

    def other(a, q):
        return full[a].at[q, pl.ds(toks, toks)]

    loads = [
        pltpu.make_async_copy(tok, block(TOK, 0), load_sem.at[0]),
        pltpu.make_async_copy(cot, block(COT, 0), load_sem.at[1]),
        pltpu.make_async_copy(w_gate, w_in.at[:, pl.ds(0, hid)], load_sem.at[2]),
        pltpu.make_async_copy(w_up, w_in.at[:, pl.ds(hid, hid)], load_sem.at[3]),
        pltpu.make_async_copy(w_down, weighted.at[pl.ds(0, hid)], load_sem.at[4]),
    ]
    for load in loads:
        load.start()
    expert_no = lax.broadcasted_iota(jnp.int32, (16, toks), 0)
    ids_all, probs_all = ids[...], probs[...].astype(F32)
    own_table = jnp.zeros((16, toks), F32)
    for k in range(ids.shape[0]):
        own_table = own_table + jnp.where(
            ids_all[k:k + 1, :] == expert_no, probs_all[k:k + 1, :], 0.0
        )
    table[...] = own_table.astype(BF16)
    barrier = pltpu.get_barrier_semaphore()
    for k in range(1, 16):
        pl.semaphore_signal(barrier, inc=1, device_id=peer(*peers[k]), device_id_type=MESH)
    pl.semaphore_signal(barrier, inc=1, device_id=y_peer, device_id_type=MESH)
    pl.semaphore_wait(barrier, 16)

    def send_core(a, q):
        send(block(a, q), other(a, q), cs_sem.at[a, q], cr_sem.at[a, q], peer(0, 0, 1))

    def send_x(a, i):
        send(block(a, 2 * i), block(a, 2 * i + 1), xs_sem.at[a, i], xr_sem.at[a, i],
             peer(0, 1, 0))

    def send_z(a, i, to, lands, n, when=None):
        send(block(a, 2 * i), block(a, 2 * lands), zs_sem.at[a, n], zr_sem.at[a, lands - 1],
             peer(to, 0, 0), when)

    for k in range(1, 16):
        send(table, meta.at[k], ms_sem.at[k], mr_sem.at[k], peer(*peers[k]))
    for a in (TOK, COT):
        loads[a].wait()
        send_core(a, 0)
        send_z(a, 0, 1, 1, 0)
        send_x(a, 0)
        send_z(a, 0, 3, 3, 1, is_mid)

    expert_row = expert_no == ep
    odd = lax.broadcasted_iota(jnp.int32, (16, toks), 0) % 2
    slot_no = lax.broadcasted_iota(jnp.int32, (m, toks), 0).astype(F32)

    def make_picks(first, last):
        for k in range(2 * first, 2 * last):
            if k:
                arrived(meta.at[k], ms_sem.at[k], mr_sem.at[k])
            named = (table[...] if k == 0 else meta[k]).astype(F32)
            p_rows[k:k + 1, :] = jnp.sum(
                jnp.where(expert_row, named, 0.0), axis=0, keepdims=True
            )
        chosen = p_rows[...] > 0.0
        before = (
            lax.broadcasted_iota(jnp.int32, (toks, toks), 0)
            < lax.broadcasted_iota(jnp.int32, (toks, toks), 1)
        )
        place = jnp.dot(
            jnp.where(chosen, 1.0, 0.0).astype(BF16), jnp.where(before, 1.0, 0.0).astype(BF16),
            preferred_element_type=F32,
        )
        place = jnp.where(chosen, place + (odd * cap).astype(F32), -1.0)
        for q in range(first, last):
            for h in range(2):
                k = 2 * q + h
                lanes = slice(h * toks, (h + 1) * toks)
                hit = slot_no == place[k:k + 1, :]
                value = jnp.where(hit, p_rows[k:k + 1, :], 0.0)
                pick[q, :, lanes] = jnp.where(hit, 1.0, 0.0).astype(BF16)
                pick_p[q, :, lanes] = value.astype(BF16)
        return place

    p_rows[...] = jnp.zeros_like(p_rows)
    make_picks(0, 1)
    across_last = (((1,), (1,)), ((), ()))
    t_w, t_h = tile_of(width, TILE_ROWS), tile_of(hid, TILE_IN)
    t_d = tile_of(width, TILE_BACK)
    t_x = tile_of(width, 256)

    def cols(n, t):
        return pl.ds(pl.multiple_of(n * t, t), t)

    across_first = (((0,), (0,)), ((), ()))

    def turn_weights():
        place = make_picks(1, 8)
        eye = (
            lax.broadcasted_iota(jnp.int32, (toks, toks), 0)
            == lax.broadcasted_iota(jnp.int32, (toks, toks), 1)
        )
        place_t[...] = lax.dot_general(
            jnp.where(eye, 1.0, 0.0).astype(BF16), place.astype(BF16), across_last,
            preferred_element_type=F32,
        )
        loads[4].wait()

        @pl.loop(0, width // t_x)
        def _(n):
            w_raw[cols(n, t_x), :] = weighted[0:hid, cols(n, t_x)].T

        @pl.loop(0, width // t_x)
        def _(n):
            w_back[:, cols(n, t_x)] = w_in[cols(n, t_x), :].T

    def do_rows(a, i, dx):
        q = 2 * i + dx
        mine = pl.ds(q * m, m)
        arrived(other(a, q), cs_sem.at[a, q], cr_sem.at[a, q])
        to = rows if a == TOK else weighted

        @pl.loop(0, width // t_w)
        def _(n):
            to[mine, cols(n, t_w)] = jnp.dot(
                pick[q], full[a][q, :, cols(n, t_w)], preferred_element_type=F32
            ).astype(BF16)

        if a == TOK:
            if q == 0:
                loads[2].wait()
                loads[3].wait()

            @pl.loop(0, 2 * hid // t_h)
            def _(n):
                part[mine, cols(n, t_h)] = jnp.dot(
                    rows[mine, :], w_in[:, cols(n, t_h)], preferred_element_type=F32
                ).astype(BF16)
        else:
            part[mine, 2 * hid:3 * hid] = jnp.dot(
                weighted[mine, :], w_raw[...], preferred_element_type=F32
            ).astype(BF16)

            @pl.loop(0, width // t_w)
            def _(n):
                weighted[mine, cols(n, t_w)] = jnp.dot(
                    pick_p[q], cs[q, :, cols(n, t_w)], preferred_element_type=F32
                ).astype(BF16)

    def across(a, q):
        at = (pl.ds(q * m, m), pl.ds(a * 2 * hid, (2 - a) * hid))
        return remote(
            part.at[at], summed.at[at], ys_sem.at[a, q], yr_sem.at[a, q], y_peer
        )

    def do_grads(i, dx):
        q = 2 * i + dx
        mine = pl.ds(q * m, m)
        across(TOK, q).wait_recv()
        across(COT, q).wait_recv()
        prob[...] = jnp.broadcast_to(
            jnp.sum(pick_p[q].astype(F32), axis=1, keepdims=True), (m, 128)
        )
        slot_at = lax.broadcasted_iota(jnp.int32, (toks, m), 1).astype(F32)
        for h in range(2):
            k = 2 * q + h
            pick_t[h * toks:(h + 1) * toks, :] = jnp.where(
                slot_at == place_t[:, k:k + 1], 1.0, 0.0
            ).astype(BF16)

        @pl.loop(0, m // 16)
        def _(r):
            at = pl.ds(pl.multiple_of(q * m + r * 16, 16), 16)
            here = pl.ds(pl.multiple_of(r * 16, 16), 16)

            def both(n):
                lanes = slice(n * hid, (n + 1) * hid)
                return part[at, lanes].astype(F32) + summed[at, lanes].astype(F32)

            gate = both(0).astype(BF16).astype(F32)
            up = both(1).astype(BF16).astype(F32)
            raw = both(2)
            sig = jax.nn.sigmoid(gate)
            act = gate * sig
            hidden = (act * up).astype(BF16)
            scaled = prob[here, :][:, :1] * raw
            grad_gate = scaled * up * sig * (1.0 + gate * (1.0 - sig))
            summed[at, 0:hid] = hidden
            summed[at, hid:2 * hid] = grad_gate.astype(BF16)
            summed[at, 2 * hid:3 * hid] = (scaled * act).astype(BF16)
            grad_p = jnp.sum(hidden.astype(F32) * raw, axis=1, keepdims=True)
            gp_col[here, :] = jnp.broadcast_to(grad_p, (16, 128))

        for h in range(2):
            k = 2 * q + h
            lanes = slice(h * toks, (h + 1) * toks)
            value = jnp.sum(
                jnp.where(pick[q, :, lanes].astype(F32) > 0.0, gp_col[...], 0.0),
                axis=0, keepdims=True,
            )
            tile = jnp.where(expert_row, jnp.broadcast_to(value, (16, toks)), 0.0).astype(BF16)
            if k == 0:
                gp_recv[0] = tile
            else:
                gp_send[k] = tile
                send(gp_send.at[k], gp_recv.at[k], gs_sem.at[k], gr_sem.at[k], peer(*peers[k]))

        @pl.loop(0, width // t_d)
        def _(n):
            back = jnp.dot(
                summed[mine, hid:3 * hid], w_back[:, cols(n, t_d)], preferred_element_type=F32
            ).astype(BF16)
            dense = jnp.dot(pick_t[...], back, preferred_element_type=F32).astype(BF16)
            cs[q, toks:2 * toks, cols(n, t_d)] = dense[:toks]
            xs[q, toks:2 * toks, cols(n, t_d)] = dense[toks:]

        send(other(TOK, q), c_recv.at[q], bcs_sem.at[q], bcr_sem.at[q], peer(0, 0, 1))

    def add_into(q, terms, out=None):
        @pl.loop(0, toks // 16)
        def _(r):
            here = pl.ds(pl.multiple_of(r * 16, 16), 16)
            mine = pl.ds(pl.multiple_of(toks + r * 16, 16), 16)
            total = cs[q, mine, :].astype(F32)
            for ref, n in terms:
                total = total + ref[n, here, :].astype(F32)
            if out is None:
                cs[q, mine, :] = total.astype(BF16)
            else:
                out[here, :] = total.astype(BF16)

    def core_arrived(q):
        arrived(c_recv.at[q], bcs_sem.at[q], bcr_sem.at[q])

    def copy_out(u, fn):
        if u < 8:
            t = width // 8
            fn(pltpu.make_async_copy(
                part.at[pl.ds(u % 4 * width // 8, t), pl.ds(0, hid)],
                out_gate.at[pl.ds(u * t, t)], out_sem.at[u % 4, 0]))
            fn(pltpu.make_async_copy(
                part.at[pl.ds(u % 4 * width // 8, t), pl.ds(hid, hid)],
                out_up.at[pl.ds(u * t, t)], out_sem.at[u % 4, 1]))
        else:
            t = hid // 3
            fn(pltpu.make_async_copy(
                part.at[pl.ds(u % 4 * width // 8, t), pl.ds(0, width)],
                out_down.at[pl.ds((u - 8) * t, t)], out_sem.at[u % 4, 0]))

    def do_weights(first, last):
        for u in range(first, last):
            if u >= 4:
                copy_out(u - 4, lambda copy: copy.wait())
            if u < 8:
                t = width // 8
                lhs, l_at, rhs, r_at, count = rows, u * t, summed, hid, 2 * hid
            else:
                t = hid // 3
                lhs, l_at, rhs, r_at, count = summed, (u - 8) * t, weighted, 0, width
            t_n = tile_of(count, TILE_OUT)

            @pl.loop(0, count // t_n)
            def _(n):
                part[u % 4 * width // 8:u % 4 * width // 8 + t, cols(n, t_n)] = lax.dot_general(
                    lhs[:, l_at:l_at + t],
                    rhs[:, pl.ds(pl.multiple_of(r_at + n * t_n, 128), t_n)],
                    across_first, preferred_element_type=F32,
                ).astype(BF16)

            copy_out(u, lambda copy: copy.start())

    for task, *which in ORDER:
        if task == "rows":
            do_rows(*which)
        elif task == "across":
            a, i, dx = which
            copy = across(a, 2 * i + dx)
            copy.start()
            y_copies.append(copy)
        elif task == "by_z":
            send(block(COT, 1), block(COT, 3), zs_sem.at[COT, 5], xr_sem.at[COT, 1],
                 peer(1, 0, 0))
        elif task == "grads":
            do_grads(*which)
        elif task == "z":
            a, i = which
            q = 2 * i
            wait = functools.partial(
                arrived, block(a, q), zs_sem.at[a, 0], zr_sem.at[a, i - 1]
            )
            if i == 3:
                pl.when(is_end)(wait)
            else:
                wait()
            if i == 1:
                send_z(a, 1, 3, 2, 2, is_mid)
            if i == 2:
                send_z(a, 2, 1, 3, 3, is_mid)
            if (a, i) != (COT, 1):
                send_x(a, i)
            send_core(a, q)
        elif task == "mid":
            a, i = which
            pl.when(is_mid)(
                functools.partial(arrived, block(a, 6), zs_sem.at[a, 0], zr_sem.at[a, 2])
            )
            send_z(a, 3, 1, 2, 4, is_mid)
        elif task == "x":
            a, i = which
            arrived(block(a, 2 * i + 1), xs_sem.at[a, i], xr_sem.at[a, i])
            send_core(a, 2 * i + 1)
        elif task == "send_x":
            (i,) = which
            q = 2 * i + 1
            core_arrived(q)
            add_into(q, [(c_recv, q)])
            send(other(COT, q), x_recv.at[i], bxs_sem.at[i], bxr_sem.at[i], peer(0, 1, 0))
        elif task == "send_z":
            (i,) = which
            core_arrived(2 * i)
            arrived(x_recv.at[i], bxs_sem.at[i], bxr_sem.at[i])
            add_into(2 * i, [(c_recv, 2 * i), (x_recv, i)])
            if i:
                send(other(COT, 2 * i), z_recv.at[i - 1], bzs_sem.at[i - 1],
                     bzr_sem.at[i - 1], peer(i, 0, 0))
        elif task == "turn":
            turn_weights()
        elif task == "weights":
            while y_copies:
                y_copies.pop().wait_send()
            do_weights(*which)
        elif task == "total":
            for n in range(3):
                arrived(z_recv.at[n], bzs_sem.at[n], bzr_sem.at[n])
            add_into(0, [(z_recv, 0), (z_recv, 1), (z_recv, 2)], out_tok)
            for k in range(1, 16):
                arrived(gp_recv.at[k], gs_sem.at[k], gr_sem.at[k])
            total = gp_recv[0].astype(F32)
            for k in range(1, 16):
                total = total + gp_recv[k].astype(F32)
            for k in range(ids.shape[0]):
                out_prob[k:k + 1, :] = jnp.sum(
                    jnp.where(ids[k:k + 1, :] == expert_no, total, 0.0), axis=0, keepdims=True
                )
    for u in range(7, 11):
        copy_out(u, lambda copy: copy.wait())
    for copy, when in pending:
        if when is None:
            copy.wait_send()
        else:
            pl.when(when)(copy.wait_send)


def hand_over_kernel(probs, *refs):
    out_probs, refs = refs[4], refs[:4] + refs[5:]
    sources, results, holds, (in_sem, out_sem) = refs[:4], refs[4:8], refs[8:12], refs[12:]
    inward, outward = [], []
    for source, result, hold, pieces in zip(sources, results, holds, PIECES):
        step = source.shape[0] // pieces
        for r in range(pieces):
            at, n = pl.ds(r * step, step), len(inward)
            inward.append(pltpu.make_async_copy(source.at[at], hold.at[at], in_sem.at[n]))
            outward.append(pltpu.make_async_copy(hold.at[at], result.at[at], out_sem.at[n]))
    for copy in inward:
        copy.start()
    out_probs[...] = probs[...].astype(BF16)
    for copy, after in zip(inward, outward):
        copy.wait()
        after.start()
    for copy in outward:
        copy.wait()


PIECES = (1, 4, 4, 4)


def hand_over(probs, *arrays):
    vmem, anywhere = pl.BlockSpec(memory_space=pltpu.VMEM), pl.BlockSpec(memory_space=pl.ANY)
    return pl.pallas_call(
        hand_over_kernel,
        out_shape=(jax.ShapeDtypeStruct(probs.shape, BF16),)
        + tuple(jax.ShapeDtypeStruct(a.shape, a.dtype) for a in arrays),
        in_specs=[vmem] + [anywhere] * 4,
        out_specs=(vmem,) + (anywhere,) * 4,
        scratch_shapes=[pltpu.VMEM(a.shape, a.dtype) for a in arrays]
        + [pltpu.SemaphoreType.DMA((sum(PIECES),))] * 2,
        compiler_params=pltpu.CompilerParams(vmem_limit_bytes=VMEM_BYTES),
        name="hand_over",
    )(probs, *arrays)


def per_device_fused(tokens, cotangent, gate_probs, expert_ids, w_gate, w_up, w_down):
    toks, top_count = expert_ids.shape
    width, hid = tokens.shape[1], w_gate.shape[2]
    cap = slot_capacity(toks, top_count, 16)
    m, slots = 2 * cap, 16 * cap
    anywhere = pl.BlockSpec(memory_space=pl.ANY)
    vmem = pl.BlockSpec(memory_space=pltpu.VMEM)
    dma = pltpu.SemaphoreType.DMA
    grad_tokens, grad_table, new_gate, new_up, new_down = pl.pallas_call(
        functools.partial(expert_kernel, cap),
        out_shape=(
            jax.ShapeDtypeStruct((toks, width), BF16),
            jax.ShapeDtypeStruct((top_count, toks), F32),
            jax.ShapeDtypeStruct((width, hid), BF16),
            jax.ShapeDtypeStruct((width, hid), BF16),
            jax.ShapeDtypeStruct((hid, width), BF16),
        ),
        in_specs=[vmem] * 2 + [anywhere] * 5,
        out_specs=(vmem, vmem, anywhere, anywhere, anywhere),
        scratch_shapes=[
            pltpu.VMEM((16, toks), BF16),
            pltpu.VMEM((8, 2 * toks, width), BF16),
            pltpu.VMEM((8, 2 * toks, width), BF16),
            pltpu.VMEM((width, 2 * hid), BF16),
            pltpu.VMEM((2 * hid, width), BF16),
            pltpu.VMEM((width, hid), BF16),
            pltpu.VMEM((slots, width), BF16),
            pltpu.VMEM((slots, width), BF16),
            pltpu.VMEM((slots, 3 * hid), BF16),
            pltpu.VMEM((slots, 3 * hid), BF16),
            pltpu.VMEM((8, toks, width), BF16),
            pltpu.VMEM((4, toks, width), BF16),
            pltpu.VMEM((3, toks, width), BF16),
            pltpu.VMEM((8, m, 2 * toks), BF16),
            pltpu.VMEM((8, m, 2 * toks), BF16),
            pltpu.VMEM((2 * toks, m), BF16),
            pltpu.VMEM((toks, 16), F32),
            pltpu.VMEM((m, 128), F32),
            pltpu.VMEM((m, 128), F32),
            pltpu.VMEM((16, 16, toks), BF16),
            pltpu.VMEM((16, 16, toks), BF16),
            pltpu.VMEM((16, 16, toks), BF16),
            pltpu.VMEM((16, toks), F32),
            dma((5,)), dma((2, 6)), dma((2, 3)), dma((2, 4)), dma((2, 4)),
            dma((2, 8)), dma((2, 8)), dma((2, 8)), dma((2, 8)),
            dma((8,)), dma((8,)), dma((4,)), dma((4,)), dma((3,)), dma((3,)),
            dma((16,)), dma((16,)), dma((16,)), dma((16,)), dma((4, 2)),
        ],
        compiler_params=pltpu.CompilerParams(
            collective_id=0, has_side_effects=True, vmem_limit_bytes=VMEM_BYTES
        ),
        name="expert_layer",
    )(expert_ids.T, gate_probs.T, tokens, cotangent, w_gate[0], w_up[0], w_down[0])
    grad_probs, grad_tokens, new_gate, new_up, new_down = hand_over(
        grad_table, grad_tokens, new_gate, new_up, new_down
    )
    grad_probs = grad_probs.T
    return (grad_tokens, grad_probs, new_gate[None], new_up[None], new_down[None])


VMEM_BYTES = 62 * 1024 * 1024


def build_slots(routing, experts, capacity):
    flat_ids = routing.reshape(-1)
    choose = (flat_ids[:, None] == jnp.arange(experts, dtype=jnp.int32)[None, :]).astype(jnp.int32)
    count = flat_ids.shape[0]
    below = jnp.tril(jnp.ones((count, count), jnp.bfloat16), -1)
    earlier = jnp.dot(
        below, choose.astype(jnp.bfloat16), preferred_element_type=jnp.float32
    ).astype(jnp.int32)
    position = jnp.sum(earlier * choose, axis=1)
    slot_of = flat_ids * capacity + position
    pair_number = jnp.arange(flat_ids.shape[0], dtype=jnp.int32) + 1
    filled_by = jnp.zeros((experts * capacity,), jnp.int32).at[slot_of].set(pair_number)
    return (slot_of, filled_by)


def activate(gate_up, hidden_units):
    gate_proj = gate_up[:, :hidden_units].astype(jnp.float32)
    up_proj = gate_up[:, hidden_units:].astype(jnp.float32)
    sigmoid_gate = jax.nn.sigmoid(gate_proj)
    gate_act = gate_proj * sigmoid_gate
    return (gate_proj, up_proj, sigmoid_gate, gate_act)


def local_grads(raw_grad, gate_up, prob_rows, hidden_units):
    gate_proj, up_proj, sigmoid_gate, gate_act = activate(gate_up, hidden_units)
    hidden = (gate_act * up_proj).astype(jnp.bfloat16)
    scaled = prob_rows.astype(jnp.float32)[:, None] * raw_grad
    grad_gate = scaled * up_proj * sigmoid_gate * (1.0 + gate_proj * (1.0 - sigmoid_gate))
    grad_up = scaled * gate_act
    grad_gate_up = jnp.concatenate(
        [grad_gate.astype(jnp.bfloat16), grad_up.astype(jnp.bfloat16)], axis=1
    )
    grad_prob = jnp.sum(hidden.astype(jnp.float32) * raw_grad, axis=1).astype(jnp.bfloat16)
    return (grad_gate_up, grad_prob)


def slot_capacity(tok_dev, top_count, experts):
    return (9 * tok_dev * top_count + 8 * experts - 1) // (8 * experts)


def per_device(tokens, cotangent, gate_probs, expert_ids, w_gate, w_up, w_down):
    arrays = (tokens, cotangent, gate_probs, expert_ids, w_gate, w_up, w_down)
    capacity = slot_capacity(expert_ids.shape[0], expert_ids.shape[1], lax.axis_size("ep"))
    if (
        lax.axis_size("fs") == 2
        and lax.axis_size("ep") == 16
        and capacity % 8 == 0
        and expert_ids.shape[0] == 128
    ):
        return per_device_fused(*arrays)
    return per_device_slots(*arrays)


def per_device_slots(tokens, cotangent, gate_probs, expert_ids, w_gate, w_up, w_down):
    tok_dev, top_count = expert_ids.shape
    experts = lax.axis_size("ep")
    shards = lax.axis_size("fs")
    width_dev = tokens.shape[1]
    hidden_units = w_gate.shape[2]
    capacity = slot_capacity(tok_dev, top_count, experts)
    slot_count = experts * capacity
    share_rows = slot_count // shards
    slot_of, filled_by = build_slots(expert_ids, experts, capacity)
    filled = filled_by > 0
    assign = jnp.maximum(filled_by - 1, 0)
    source_token = assign // top_count
    token_send = jnp.where(
        filled[:, None], jnp.take(tokens, source_token, axis=0), jnp.zeros((), tokens.dtype)
    ).reshape(experts, capacity, width_dev)
    grad_send = jnp.where(
        filled[:, None], jnp.take(cotangent, source_token, axis=0), jnp.zeros((), cotangent.dtype)
    ).reshape(experts, capacity, width_dev)
    prob_send = jnp.where(
        filled, jnp.take(gate_probs.reshape(-1), assign, axis=0), jnp.zeros((), gate_probs.dtype)
    ).reshape(experts, capacity)
    token_recv = lax.all_to_all(token_send, "ep", split_axis=0, concat_axis=0, tiled=True)
    token_rows = token_recv.reshape(slot_count, width_dev)
    stacked = jnp.concatenate([w_gate[0], w_up[0]], axis=1)
    down_local = w_down[0]
    section = token_rows
    summed = lax.psum(
        jnp.dot(section, stacked, preferred_element_type=jnp.float32).astype(jnp.bfloat16), "fs"
    )
    gate_up = lax.optimization_barrier(summed)
    gate_proj, up_proj, sigmoid_gate, gate_act = activate(gate_up, hidden_units)
    hidden = (gate_act * up_proj).astype(jnp.bfloat16)
    grad_recv, prob_recv = (
        lax.all_to_all(grad_send, "ep", split_axis=0, concat_axis=0, tiled=True),
        lax.all_to_all(prob_send, "ep", split_axis=0, concat_axis=0, tiled=True),
    )
    grad_rows = grad_recv.reshape(slot_count, width_dev)
    prob_rows = prob_recv.reshape(slot_count)
    weighted = (prob_rows.astype(jnp.float32)[:, None] * grad_rows.astype(jnp.float32)).astype(
        jnp.bfloat16
    )
    across_last = (((1,), (1,)), ((), ()))
    across_first = (((0,), (0,)), ((), ()))
    section = grad_rows
    raw_share = lax.psum_scatter(
        lax.dot_general(
            section, down_local, across_last, preferred_element_type=jnp.float32
        ).astype(jnp.bfloat16),
        "fs",
        scatter_dimension=0,
        tiled=True,
    ).astype(jnp.float32)
    first_row = lax.axis_index("fs") * share_rows
    share_gate_up = lax.dynamic_slice_in_dim(gate_up, first_row, share_rows, 0)
    share_prob_rows = lax.dynamic_slice_in_dim(prob_rows, first_row, share_rows, 0)
    share_grads, share_probs = local_grads(raw_share, share_gate_up, share_prob_rows, hidden_units)
    grad_gate_up, grad_prob = (
        lax.all_gather(share_grads, "fs", axis=0, tiled=True),
        lax.all_gather(share_probs, "fs", axis=0, tiled=True),
    )
    new_down = lax.dot_general(
        hidden, weighted, across_first, preferred_element_type=jnp.float32
    ).astype(jnp.bfloat16)
    joint = lax.dot_general(
        token_rows, grad_gate_up, across_first, preferred_element_type=jnp.float32
    ).astype(jnp.bfloat16)
    new_gate = joint[:, :hidden_units]
    new_up = joint[:, hidden_units:]
    grad_part = lax.dot_general(
        grad_gate_up, stacked, across_last, preferred_element_type=jnp.float32
    ).astype(jnp.bfloat16)
    part_back, prob_back = (
        lax.all_to_all(
            grad_part.reshape(experts, capacity, width_dev),
            "ep",
            split_axis=0,
            concat_axis=0,
            tiled=True,
        ),
        lax.all_to_all(
            grad_prob.reshape(experts, capacity), "ep", split_axis=0, concat_axis=0, tiled=True
        ),
    )
    returned = jnp.take(part_back.reshape(slot_count, width_dev), slot_of, axis=0)
    grad_tokens = jnp.sum(
        returned.reshape(tok_dev, top_count, width_dev).astype(jnp.float32), axis=1
    ).astype(jnp.bfloat16)
    grad_probs = jnp.take(prob_back.reshape(slot_count), slot_of, axis=0).reshape(
        tok_dev, top_count
    )
    return (grad_tokens, grad_probs, new_gate[None], new_up[None], new_down[None])


def solution(mesh):
    return jax.shard_map(
        per_device,
        mesh=mesh,
        in_specs=(
            P("ep", "fs"),
            P("ep", "fs"),
            P("ep", None),
            P("ep", None),
            P("ep", "fs", None),
            P("ep", "fs", None),
            P("ep", None, "fs"),
        ),
        out_specs=(
            P("ep", "fs"),
            P("ep", None),
            P("ep", "fs", None),
            P("ep", "fs", None),
            P("ep", None, "fs"),
        ),
        check_vma=False,
    )
```

```python
import functools

import jax
import jax.numpy as jnp
from jax import lax
from jax.experimental import pallas as pl
from jax.experimental.pallas import tpu as pltpu
from jax.sharding import PartitionSpec as P

BF16, F32 = jnp.bfloat16, jnp.float32
MESH = pl.DeviceIdType.MESH
TOK, COT = 0, 1
TILE_ROWS, TILE_IN, TILE_BACK, TILE_OUT = 1024, 768, 1024, 1024
ORDER = [
    ("rows", TOK, 0, 0),
    ("across", TOK, 0, 0),
    ("turn",),
    ("z", TOK, 1),
    ("mid", TOK, 3),
    ("x", TOK, 0),
    ("rows", TOK, 0, 1),
    ("across", TOK, 0, 1),
    ("rows", TOK, 1, 0),
    ("across", TOK, 1, 0),
    ("z", COT, 1),
    ("mid", COT, 3),
    ("x", COT, 0),
    ("rows", COT, 1, 0),
    ("across", COT, 1, 0),
    ("rows", COT, 0, 1),
    ("rows", COT, 0, 0),
    ("z", TOK, 2),
    ("x", TOK, 1),
    ("rows", TOK, 1, 1),
    ("across", TOK, 1, 1),
    ("rows", TOK, 2, 0),
    ("across", TOK, 2, 0),
    ("grads", 1, 0),
    ("z", COT, 2),
    ("x", TOK, 2),
    ("rows", TOK, 2, 1),
    ("across", TOK, 2, 1),
    ("rows", COT, 2, 0),
    ("across", COT, 2, 0),
    ("z", TOK, 3),
    ("x", COT, 2),
    ("rows", COT, 2, 1),
    ("across", COT, 2, 1),
    ("z", COT, 3),
    ("by_z",),
    ("x", TOK, 3),
    ("rows", TOK, 3, 1),
    ("across", TOK, 3, 1),
    ("grads", 2, 0),
    ("x", COT, 3),
    ("rows", COT, 3, 1),
    ("across", COT, 3, 1),
    ("grads", 2, 1),
    ("send_x", 2),
    ("rows", TOK, 3, 0),
    ("across", TOK, 3, 0),
    ("rows", COT, 3, 0),
    ("across", COT, 3, 0),
    ("x", COT, 1),
    ("rows", COT, 1, 1),
    ("across", COT, 1, 1),
    ("across", COT, 0, 1),
    ("across", COT, 0, 0),
    ("send_z", 2, 0),
    ("send_z", 2, 1),
    ("grads", 3, 1),
    ("send_x", 3),
    ("grads", 3, 0),
    ("grads", 1, 1),
    ("send_x", 1),
    ("send_z", 3, 0),
    ("grads", 0, 1),
    ("send_x", 0),
    ("send_z", 3, 1),
    ("grads", 0, 0),
    ("weights", 0, 1),
    ("send_z", 1, 0),
    ("weights", 1, 4),
    ("send_z", 1, 1),
    ("weights", 4, 11),
    ("send_z", 0, 0),
    ("send_z", 0, 1),
    ("total",),
]


def tile_of(size, most):
    while size % most:
        most //= 2
    return most


def expert_kernel(
    cap, ids, probs, tok, cot, w_gate, w_up, w_down,
    out_tok, out_prob, out_gate, out_up, out_down,
    table, xs, cs, w_in, w_back, w_raw, rows, weighted, part, summed, c_recv, x_recv, z_recv,
    pick, pick_p, pick_t, place_t, prob, gp_col, meta, gp_send, gp_recv, p_rows,
    load_sem, zs_sem, zr_sem, xs_sem, xr_sem, cs_sem, cr_sem, ys_sem, yr_sem,
    bcs_sem, bcr_sem, bxs_sem, bxr_sem, bzs_sem, bzr_sem,
    ms_sem, mr_sem, gs_sem, gr_sem, out_sem,
):
    toks, width = tok.shape
    hid = w_gate.shape[1]
    m = 2 * cap
    ep, fs = lax.axis_index("ep"), lax.axis_index("fs")
    z, x, c = ep // 4, (ep // 2) % 2, ep % 2
    z_of = (z, z + 1 - 2 * (z % 2), (z + 2) % 4, 3 - z)
    x_of, c_of = (x, 1 - x), (c, 1 - c)
    is_mid = jnp.logical_or(z == 1, z == 2)
    is_end = jnp.logical_not(is_mid)
    full = (xs, cs)

    def peer(i, dx, dc):
        return ((z_of[i] * 2 + x_of[dx]) * 2 + c_of[dc], fs)

    y_peer = (ep, 1 - fs)
    peers = [(k // 4, (k // 2) % 2, k % 2) for k in range(16)]
    pending, y_copies = [], []

    def remote(src, dst, ssem, rsem, dev):
        return pltpu.make_async_remote_copy(
            src_ref=src, dst_ref=dst, send_sem=ssem, recv_sem=rsem,
            device_id=dev, device_id_type=MESH,
        )

    def send(src, dst, ssem, rsem, dev, when=None):
        copy = remote(src, dst, ssem, rsem, dev)
        pending.append((copy, when))
        if when is None:
            copy.start()
        else:
            pl.when(when)(copy.start)

    def arrived(dst, ssem, rsem):
        remote(dst, dst, ssem, rsem, y_peer).wait_recv()

    def block(a, q):
        return full[a].at[q, pl.ds(0, toks)]

    def other(a, q):
        return full[a].at[q, pl.ds(toks, toks)]

    loads = [
        pltpu.make_async_copy(tok, block(TOK, 0), load_sem.at[0]),
        pltpu.make_async_copy(cot, block(COT, 0), load_sem.at[1]),
        pltpu.make_async_copy(w_gate, w_in.at[:, pl.ds(0, hid)], load_sem.at[2]),
        pltpu.make_async_copy(w_up, w_in.at[:, pl.ds(hid, hid)], load_sem.at[3]),
        pltpu.make_async_copy(w_down, weighted.at[pl.ds(0, hid)], load_sem.at[4]),
    ]
    for load in loads:
        load.start()
    expert_no = lax.broadcasted_iota(jnp.int32, (16, toks), 0)
    ids_all, probs_all = ids[...], probs[...].astype(F32)
    own_table = jnp.zeros((16, toks), F32)
    for k in range(ids.shape[0]):
        own_table = own_table + jnp.where(
            ids_all[k:k + 1, :] == expert_no, probs_all[k:k + 1, :], 0.0
        )
    table[...] = own_table.astype(BF16)
    barrier = pltpu.get_barrier_semaphore()
    for k in range(1, 16):
        pl.semaphore_signal(barrier, inc=1, device_id=peer(*peers[k]), device_id_type=MESH)
    pl.semaphore_signal(barrier, inc=1, device_id=y_peer, device_id_type=MESH)
    pl.semaphore_wait(barrier, 16)

    def send_core(a, q):
        send(block(a, q), other(a, q), cs_sem.at[a, q], cr_sem.at[a, q], peer(0, 0, 1))

    def send_x(a, i):
        send(block(a, 2 * i), block(a, 2 * i + 1), xs_sem.at[a, i], xr_sem.at[a, i],
             peer(0, 1, 0))

    def send_z(a, i, to, lands, n, when=None):
        send(block(a, 2 * i), block(a, 2 * lands), zs_sem.at[a, n], zr_sem.at[a, lands - 1],
             peer(to, 0, 0), when)

    for k in range(1, 16):
        send(table, meta.at[k], ms_sem.at[k], mr_sem.at[k], peer(*peers[k]))
    for a in (TOK, COT):
        loads[a].wait()
        send_core(a, 0)
        send_z(a, 0, 1, 1, 0)
        send_x(a, 0)
        send_z(a, 0, 3, 3, 1, is_mid)

    expert_row = expert_no == ep
    odd = lax.broadcasted_iota(jnp.int32, (16, toks), 0) % 2
    slot_no = lax.broadcasted_iota(jnp.int32, (m, toks), 0).astype(F32)

    def make_picks(first, last):
        for k in range(2 * first, 2 * last):
            if k:
                arrived(meta.at[k], ms_sem.at[k], mr_sem.at[k])
            named = (table[...] if k == 0 else meta[k]).astype(F32)
            p_rows[k:k + 1, :] = jnp.sum(
                jnp.where(expert_row, named, 0.0), axis=0, keepdims=True
            )
        chosen = p_rows[...] > 0.0
        before = (
            lax.broadcasted_iota(jnp.int32, (toks, toks), 0)
            < lax.broadcasted_iota(jnp.int32, (toks, toks), 1)
        )
        place = jnp.dot(
            jnp.where(chosen, 1.0, 0.0).astype(BF16), jnp.where(before, 1.0, 0.0).astype(BF16),
            preferred_element_type=F32,
        )
        place = jnp.where(chosen, place + (odd * cap).astype(F32), -1.0)
        for q in range(first, last):
            for h in range(2):
                k = 2 * q + h
                lanes = slice(h * toks, (h + 1) * toks)
                hit = slot_no == place[k:k + 1, :]
                value = jnp.where(hit, p_rows[k:k + 1, :], 0.0)
                pick[q, :, lanes] = jnp.where(hit, 1.0, 0.0).astype(BF16)
                pick_p[q, :, lanes] = value.astype(BF16)
        return place

    p_rows[...] = jnp.zeros_like(p_rows)
    make_picks(0, 1)
    across_last = (((1,), (1,)), ((), ()))
    t_w, t_h = tile_of(width, TILE_ROWS), tile_of(hid, TILE_IN)
    t_d = tile_of(width, TILE_BACK)
    t_x = tile_of(width, 256)

    def cols(n, t):
        return pl.ds(pl.multiple_of(n * t, t), t)

    across_first = (((0,), (0,)), ((), ()))

    def turn_weights():
        place = make_picks(1, 8)
        eye = (
            lax.broadcasted_iota(jnp.int32, (toks, toks), 0)
            == lax.broadcasted_iota(jnp.int32, (toks, toks), 1)
        )
        place_t[...] = lax.dot_general(
            jnp.where(eye, 1.0, 0.0).astype(BF16), place.astype(BF16), across_last,
            preferred_element_type=F32,
        )
        loads[4].wait()

        @pl.loop(0, width // t_x)
        def _(n):
            w_raw[cols(n, t_x), :] = weighted[0:hid, cols(n, t_x)].T

        @pl.loop(0, width // t_x)
        def _(n):
            w_back[:, cols(n, t_x)] = w_in[cols(n, t_x), :].T

    def do_rows(a, i, dx):
        q = 2 * i + dx
        mine = pl.ds(q * m, m)
        arrived(other(a, q), cs_sem.at[a, q], cr_sem.at[a, q])
        to = rows if a == TOK else weighted

        @pl.loop(0, width // t_w)
        def _(n):
            to[mine, cols(n, t_w)] = jnp.dot(
                pick[q], full[a][q, :, cols(n, t_w)], preferred_element_type=F32
            ).astype(BF16)

        if a == TOK:
            if q == 0:
                loads[2].wait()
                loads[3].wait()

            @pl.loop(0, 2 * hid // t_h)
            def _(n):
                part[mine, cols(n, t_h)] = jnp.dot(
                    rows[mine, :], w_in[:, cols(n, t_h)], preferred_element_type=F32
                ).astype(BF16)
        else:
            part[mine, 2 * hid:3 * hid] = jnp.dot(
                weighted[mine, :], w_raw[...], preferred_element_type=F32
            ).astype(BF16)

            @pl.loop(0, width // t_w)
            def _(n):
                weighted[mine, cols(n, t_w)] = jnp.dot(
                    pick_p[q], cs[q, :, cols(n, t_w)], preferred_element_type=F32
                ).astype(BF16)

    def across(a, q):
        at = (pl.ds(q * m, m), pl.ds(a * 2 * hid, (2 - a) * hid))
        return remote(
            part.at[at], summed.at[at], ys_sem.at[a, q], yr_sem.at[a, q], y_peer
        )

    def do_grads(i, dx):
        q = 2 * i + dx
        mine = pl.ds(q * m, m)
        across(TOK, q).wait_recv()
        across(COT, q).wait_recv()
        prob[...] = jnp.broadcast_to(
            jnp.sum(pick_p[q].astype(F32), axis=1, keepdims=True), (m, 128)
        )
        slot_at = lax.broadcasted_iota(jnp.int32, (toks, m), 1).astype(F32)
        for h in range(2):
            k = 2 * q + h
            pick_t[h * toks:(h + 1) * toks, :] = jnp.where(
                slot_at == place_t[:, k:k + 1], 1.0, 0.0
            ).astype(BF16)

        @pl.loop(0, m // 16)
        def _(r):
            at = pl.ds(pl.multiple_of(q * m + r * 16, 16), 16)
            here = pl.ds(pl.multiple_of(r * 16, 16), 16)

            def both(n):
                lanes = slice(n * hid, (n + 1) * hid)
                return part[at, lanes].astype(F32) + summed[at, lanes].astype(F32)

            gate = both(0).astype(BF16).astype(F32)
            up = both(1).astype(BF16).astype(F32)
            raw = both(2)
            sig = jax.nn.sigmoid(gate)
            act = gate * sig
            hidden = (act * up).astype(BF16)
            scaled = prob[here, :][:, :1] * raw
            grad_gate = scaled * up * sig * (1.0 + gate * (1.0 - sig))
            summed[at, 0:hid] = hidden
            summed[at, hid:2 * hid] = grad_gate.astype(BF16)
            summed[at, 2 * hid:3 * hid] = (scaled * act).astype(BF16)
            grad_p = jnp.sum(hidden.astype(F32) * raw, axis=1, keepdims=True)
            gp_col[here, :] = jnp.broadcast_to(grad_p, (16, 128))

        for h in range(2):
            k = 2 * q + h
            lanes = slice(h * toks, (h + 1) * toks)
            value = jnp.sum(
                jnp.where(pick[q, :, lanes].astype(F32) > 0.0, gp_col[...], 0.0),
                axis=0, keepdims=True,
            )
            tile = jnp.where(expert_row, jnp.broadcast_to(value, (16, toks)), 0.0).astype(BF16)
            if k == 0:
                gp_recv[0] = tile
            else:
                gp_send[k] = tile
                send(gp_send.at[k], gp_recv.at[k], gs_sem.at[k], gr_sem.at[k], peer(*peers[k]))

        @pl.loop(0, width // t_d)
        def _(n):
            back = jnp.dot(
                summed[mine, hid:3 * hid], w_back[:, cols(n, t_d)], preferred_element_type=F32
            ).astype(BF16)
            dense = jnp.dot(pick_t[...], back, preferred_element_type=F32).astype(BF16)
            cs[q, toks:2 * toks, cols(n, t_d)] = dense[:toks]
            xs[q, toks:2 * toks, cols(n, t_d)] = dense[toks:]

        send(other(TOK, q), c_recv.at[q], bcs_sem.at[q], bcr_sem.at[q], peer(0, 0, 1))

    half = toks // 2

    def part_of(ref, h):
        return ref.at[pl.ds(h * half, half)]

    def add_into(q, terms, out=None, first=0, last=toks):
        @pl.loop(first // 16, last // 16)
        def _(r):
            here = pl.ds(pl.multiple_of(r * 16, 16), 16)
            mine = pl.ds(pl.multiple_of(toks + r * 16, 16), 16)
            total = cs[q, mine, :].astype(F32)
            for ref, n in terms:
                total = total + ref[n, here, :].astype(F32)
            if out is None:
                cs[q, mine, :] = total.astype(BF16)
            else:
                out[here, :] = total.astype(BF16)

    def core_arrived(q):
        arrived(c_recv.at[q], bcs_sem.at[q], bcr_sem.at[q])

    def copy_out(u, fn):
        if u < 8:
            t = width // 8
            fn(pltpu.make_async_copy(
                part.at[pl.ds(u % 4 * width // 8, t), pl.ds(0, hid)],
                out_gate.at[pl.ds(u * t, t)], out_sem.at[u % 4, 0]))
            fn(pltpu.make_async_copy(
                part.at[pl.ds(u % 4 * width // 8, t), pl.ds(hid, hid)],
                out_up.at[pl.ds(u * t, t)], out_sem.at[u % 4, 1]))
        else:
            t = hid // 3
            fn(pltpu.make_async_copy(
                part.at[pl.ds(u % 4 * width // 8, t), pl.ds(0, width)],
                out_down.at[pl.ds((u - 8) * t, t)], out_sem.at[u % 4, 0]))

    def do_weights(first, last):
        for u in range(first, last):
            if u >= 4:
                copy_out(u - 4, lambda copy: copy.wait())
            if u < 8:
                t = width // 8
                lhs, l_at, rhs, r_at, count = rows, u * t, summed, hid, 2 * hid
            else:
                t = hid // 3
                lhs, l_at, rhs, r_at, count = summed, (u - 8) * t, weighted, 0, width
            t_n = tile_of(count, TILE_OUT)

            @pl.loop(0, count // t_n)
            def _(n):
                part[u % 4 * width // 8:u % 4 * width // 8 + t, cols(n, t_n)] = lax.dot_general(
                    lhs[:, l_at:l_at + t],
                    rhs[:, pl.ds(pl.multiple_of(r_at + n * t_n, 128), t_n)],
                    across_first, preferred_element_type=F32,
                ).astype(BF16)

            copy_out(u, lambda copy: copy.start())

    for task, *which in ORDER:
        if task == "rows":
            do_rows(*which)
        elif task == "across":
            a, i, dx = which
            copy = across(a, 2 * i + dx)
            copy.start()
            y_copies.append(copy)
        elif task == "by_z":
            send(block(COT, 1), block(COT, 3), zs_sem.at[COT, 5], xr_sem.at[COT, 1],
                 peer(1, 0, 0))
        elif task == "grads":
            do_grads(*which)
        elif task == "z":
            a, i = which
            q = 2 * i
            wait = functools.partial(
                arrived, block(a, q), zs_sem.at[a, 0], zr_sem.at[a, i - 1]
            )
            if i == 3:
                pl.when(is_end)(wait)
            else:
                wait()
            if i == 1:
                send_z(a, 1, 3, 2, 2, is_mid)
            if i == 2:
                send_z(a, 2, 1, 3, 3, is_mid)
            if (a, i) != (COT, 1):
                send_x(a, i)
            send_core(a, q)
        elif task == "mid":
            a, i = which
            pl.when(is_mid)(
                functools.partial(arrived, block(a, 6), zs_sem.at[a, 0], zr_sem.at[a, 2])
            )
            send_z(a, 3, 1, 2, 4, is_mid)
        elif task == "x":
            a, i = which
            arrived(block(a, 2 * i + 1), xs_sem.at[a, i], xr_sem.at[a, i])
            send_core(a, 2 * i + 1)
        elif task == "send_x":
            (i,) = which
            q = 2 * i + 1
            core_arrived(q)
            add_into(q, [(c_recv, q)])
            for h in range(2):
                send(part_of(other(COT, q), h), part_of(x_recv.at[i], h), bxs_sem.at[i, h],
                     bxr_sem.at[i, h], peer(0, 1, 0))
        elif task == "send_z":
            i, h = which
            if h == 0:
                core_arrived(2 * i)
            arrived(part_of(x_recv.at[i], h), bxs_sem.at[i, h], bxr_sem.at[i, h])
            add_into(2 * i, [(c_recv, 2 * i), (x_recv, i)], None, h * half, h * half + half)
            if i:
                send(part_of(other(COT, 2 * i), h), part_of(z_recv.at[i - 1], h),
                     bzs_sem.at[i - 1, h], bzr_sem.at[i - 1, h], peer(i, 0, 0))
        elif task == "turn":
            turn_weights()
        elif task == "weights":
            while y_copies:
                y_copies.pop().wait_send()
            do_weights(*which)
        elif task == "total":
            for n in range(3):
                for h in range(2):
                    arrived(part_of(z_recv.at[n], h), bzs_sem.at[n, h], bzr_sem.at[n, h])
            add_into(0, [(z_recv, 0), (z_recv, 1), (z_recv, 2)], out_tok)
            for k in range(1, 16):
                arrived(gp_recv.at[k], gs_sem.at[k], gr_sem.at[k])
            total = gp_recv[0].astype(F32)
            for k in range(1, 16):
                total = total + gp_recv[k].astype(F32)
            for k in range(ids.shape[0]):
                out_prob[k:k + 1, :] = jnp.sum(
                    jnp.where(ids[k:k + 1, :] == expert_no, total, 0.0), axis=0, keepdims=True
                )
    for u in range(7, 11):
        copy_out(u, lambda copy: copy.wait())
    for copy, when in pending:
        if when is None:
            copy.wait_send()
        else:
            pl.when(when)(copy.wait_send)


def hand_over_kernel(probs, *refs):
    out_probs, refs = refs[4], refs[:4] + refs[5:]
    sources, results, holds, (in_sem, out_sem) = refs[:4], refs[4:8], refs[8:12], refs[12:]
    inward, outward = [], []
    for source, result, hold, pieces in zip(sources, results, holds, PIECES):
        step = source.shape[0] // pieces
        for r in range(pieces):
            at, n = pl.ds(r * step, step), len(inward)
            inward.append(pltpu.make_async_copy(source.at[at], hold.at[at], in_sem.at[n]))
            outward.append(pltpu.make_async_copy(hold.at[at], result.at[at], out_sem.at[n]))
    for copy in inward:
        copy.start()
    out_probs[...] = probs[...].astype(BF16)
    for copy, after in zip(inward, outward):
        copy.wait()
        after.start()
    for copy in outward:
        copy.wait()


PIECES = (1, 4, 4, 4)


def hand_over(probs, *arrays):
    vmem, anywhere = pl.BlockSpec(memory_space=pltpu.VMEM), pl.BlockSpec(memory_space=pl.ANY)
    return pl.pallas_call(
        hand_over_kernel,
        out_shape=(jax.ShapeDtypeStruct(probs.shape, BF16),)
        + tuple(jax.ShapeDtypeStruct(a.shape, a.dtype) for a in arrays),
        in_specs=[vmem] + [anywhere] * 4,
        out_specs=(vmem,) + (anywhere,) * 4,
        scratch_shapes=[pltpu.VMEM(a.shape, a.dtype) for a in arrays]
        + [pltpu.SemaphoreType.DMA((sum(PIECES),))] * 2,
        compiler_params=pltpu.CompilerParams(vmem_limit_bytes=VMEM_BYTES),
        name="hand_over",
    )(probs, *arrays)


def per_device_fused(tokens, cotangent, gate_probs, expert_ids, w_gate, w_up, w_down):
    toks, top_count = expert_ids.shape
    width, hid = tokens.shape[1], w_gate.shape[2]
    cap = slot_capacity(toks, top_count, 16)
    m, slots = 2 * cap, 16 * cap
    anywhere = pl.BlockSpec(memory_space=pl.ANY)
    vmem = pl.BlockSpec(memory_space=pltpu.VMEM)
    dma = pltpu.SemaphoreType.DMA
    grad_tokens, grad_table, new_gate, new_up, new_down = pl.pallas_call(
        functools.partial(expert_kernel, cap),
        out_shape=(
            jax.ShapeDtypeStruct((toks, width), BF16),
            jax.ShapeDtypeStruct((top_count, toks), F32),
            jax.ShapeDtypeStruct((width, hid), BF16),
            jax.ShapeDtypeStruct((width, hid), BF16),
            jax.ShapeDtypeStruct((hid, width), BF16),
        ),
        in_specs=[vmem] * 2 + [anywhere] * 5,
        out_specs=(vmem, vmem, anywhere, anywhere, anywhere),
        scratch_shapes=[
            pltpu.VMEM((16, toks), BF16),
            pltpu.VMEM((8, 2 * toks, width), BF16),
            pltpu.VMEM((8, 2 * toks, width), BF16),
            pltpu.VMEM((width, 2 * hid), BF16),
            pltpu.VMEM((2 * hid, width), BF16),
            pltpu.VMEM((width, hid), BF16),
            pltpu.VMEM((slots, width), BF16),
            pltpu.VMEM((slots, width), BF16),
            pltpu.VMEM((slots, 3 * hid), BF16),
            pltpu.VMEM((slots, 3 * hid), BF16),
            pltpu.VMEM((8, toks, width), BF16),
            pltpu.VMEM((4, toks, width), BF16),
            pltpu.VMEM((3, toks, width), BF16),
            pltpu.VMEM((8, m, 2 * toks), BF16),
            pltpu.VMEM((8, m, 2 * toks), BF16),
            pltpu.VMEM((2 * toks, m), BF16),
            pltpu.VMEM((toks, 16), F32),
            pltpu.VMEM((m, 128), F32),
            pltpu.VMEM((m, 128), F32),
            pltpu.VMEM((16, 16, toks), BF16),
            pltpu.VMEM((16, 16, toks), BF16),
            pltpu.VMEM((16, 16, toks), BF16),
            pltpu.VMEM((16, toks), F32),
            dma((5,)), dma((2, 6)), dma((2, 3)), dma((2, 4)), dma((2, 4)),
            dma((2, 8)), dma((2, 8)), dma((2, 8)), dma((2, 8)),
            dma((8,)), dma((8,)), dma((4, 2)), dma((4, 2)), dma((3, 2)), dma((3, 2)),
            dma((16,)), dma((16,)), dma((16,)), dma((16,)), dma((4, 2)),
        ],
        compiler_params=pltpu.CompilerParams(
            collective_id=0, has_side_effects=True, vmem_limit_bytes=VMEM_BYTES
        ),
        name="expert_layer",
    )(expert_ids.T, gate_probs.T, tokens, cotangent, w_gate[0], w_up[0], w_down[0])
    grad_probs, grad_tokens, new_gate, new_up, new_down = hand_over(
        grad_table, grad_tokens, new_gate, new_up, new_down
    )
    grad_probs = grad_probs.T
    return (grad_tokens, grad_probs, new_gate[None], new_up[None], new_down[None])


VMEM_BYTES = 62 * 1024 * 1024


def build_slots(routing, experts, capacity):
    flat_ids = routing.reshape(-1)
    choose = (flat_ids[:, None] == jnp.arange(experts, dtype=jnp.int32)[None, :]).astype(jnp.int32)
    count = flat_ids.shape[0]
    below = jnp.tril(jnp.ones((count, count), jnp.bfloat16), -1)
    earlier = jnp.dot(
        below, choose.astype(jnp.bfloat16), preferred_element_type=jnp.float32
    ).astype(jnp.int32)
    position = jnp.sum(earlier * choose, axis=1)
    slot_of = flat_ids * capacity + position
    pair_number = jnp.arange(flat_ids.shape[0], dtype=jnp.int32) + 1
    filled_by = jnp.zeros((experts * capacity,), jnp.int32).at[slot_of].set(pair_number)
    return (slot_of, filled_by)


def activate(gate_up, hidden_units):
    gate_proj = gate_up[:, :hidden_units].astype(jnp.float32)
    up_proj = gate_up[:, hidden_units:].astype(jnp.float32)
    sigmoid_gate = jax.nn.sigmoid(gate_proj)
    gate_act = gate_proj * sigmoid_gate
    return (gate_proj, up_proj, sigmoid_gate, gate_act)


def local_grads(raw_grad, gate_up, prob_rows, hidden_units):
    gate_proj, up_proj, sigmoid_gate, gate_act = activate(gate_up, hidden_units)
    hidden = (gate_act * up_proj).astype(jnp.bfloat16)
    scaled = prob_rows.astype(jnp.float32)[:, None] * raw_grad
    grad_gate = scaled * up_proj * sigmoid_gate * (1.0 + gate_proj * (1.0 - sigmoid_gate))
    grad_up = scaled * gate_act
    grad_gate_up = jnp.concatenate(
        [grad_gate.astype(jnp.bfloat16), grad_up.astype(jnp.bfloat16)], axis=1
    )
    grad_prob = jnp.sum(hidden.astype(jnp.float32) * raw_grad, axis=1).astype(jnp.bfloat16)
    return (grad_gate_up, grad_prob)


def slot_capacity(tok_dev, top_count, experts):
    return (9 * tok_dev * top_count + 8 * experts - 1) // (8 * experts)


def per_device(tokens, cotangent, gate_probs, expert_ids, w_gate, w_up, w_down):
    arrays = (tokens, cotangent, gate_probs, expert_ids, w_gate, w_up, w_down)
    capacity = slot_capacity(expert_ids.shape[0], expert_ids.shape[1], lax.axis_size("ep"))
    if (
        lax.axis_size("fs") == 2
        and lax.axis_size("ep") == 16
        and capacity % 8 == 0
        and expert_ids.shape[0] == 128
    ):
        return per_device_fused(*arrays)
    return per_device_slots(*arrays)


def per_device_slots(tokens, cotangent, gate_probs, expert_ids, w_gate, w_up, w_down):
    tok_dev, top_count = expert_ids.shape
    experts = lax.axis_size("ep")
    shards = lax.axis_size("fs")
    width_dev = tokens.shape[1]
    hidden_units = w_gate.shape[2]
    capacity = slot_capacity(tok_dev, top_count, experts)
    slot_count = experts * capacity
    share_rows = slot_count // shards
    slot_of, filled_by = build_slots(expert_ids, experts, capacity)
    filled = filled_by > 0
    assign = jnp.maximum(filled_by - 1, 0)
    source_token = assign // top_count
    token_send = jnp.where(
        filled[:, None], jnp.take(tokens, source_token, axis=0), jnp.zeros((), tokens.dtype)
    ).reshape(experts, capacity, width_dev)
    grad_send = jnp.where(
        filled[:, None], jnp.take(cotangent, source_token, axis=0), jnp.zeros((), cotangent.dtype)
    ).reshape(experts, capacity, width_dev)
    prob_send = jnp.where(
        filled, jnp.take(gate_probs.reshape(-1), assign, axis=0), jnp.zeros((), gate_probs.dtype)
    ).reshape(experts, capacity)
    token_recv = lax.all_to_all(token_send, "ep", split_axis=0, concat_axis=0, tiled=True)
    token_rows = token_recv.reshape(slot_count, width_dev)
    stacked = jnp.concatenate([w_gate[0], w_up[0]], axis=1)
    down_local = w_down[0]
    section = token_rows
    summed = lax.psum(
        jnp.dot(section, stacked, preferred_element_type=jnp.float32).astype(jnp.bfloat16), "fs"
    )
    gate_up = lax.optimization_barrier(summed)
    gate_proj, up_proj, sigmoid_gate, gate_act = activate(gate_up, hidden_units)
    hidden = (gate_act * up_proj).astype(jnp.bfloat16)
    grad_recv, prob_recv = (
        lax.all_to_all(grad_send, "ep", split_axis=0, concat_axis=0, tiled=True),
        lax.all_to_all(prob_send, "ep", split_axis=0, concat_axis=0, tiled=True),
    )
    grad_rows = grad_recv.reshape(slot_count, width_dev)
    prob_rows = prob_recv.reshape(slot_count)
    weighted = (prob_rows.astype(jnp.float32)[:, None] * grad_rows.astype(jnp.float32)).astype(
        jnp.bfloat16
    )
    across_last = (((1,), (1,)), ((), ()))
    across_first = (((0,), (0,)), ((), ()))
    section = grad_rows
    raw_share = lax.psum_scatter(
        lax.dot_general(
            section, down_local, across_last, preferred_element_type=jnp.float32
        ).astype(jnp.bfloat16),
        "fs",
        scatter_dimension=0,
        tiled=True,
    ).astype(jnp.float32)
    first_row = lax.axis_index("fs") * share_rows
    share_gate_up = lax.dynamic_slice_in_dim(gate_up, first_row, share_rows, 0)
    share_prob_rows = lax.dynamic_slice_in_dim(prob_rows, first_row, share_rows, 0)
    share_grads, share_probs = local_grads(raw_share, share_gate_up, share_prob_rows, hidden_units)
    grad_gate_up, grad_prob = (
        lax.all_gather(share_grads, "fs", axis=0, tiled=True),
        lax.all_gather(share_probs, "fs", axis=0, tiled=True),
    )
    new_down = lax.dot_general(
        hidden, weighted, across_first, preferred_element_type=jnp.float32
    ).astype(jnp.bfloat16)
    joint = lax.dot_general(
        token_rows, grad_gate_up, across_first, preferred_element_type=jnp.float32
    ).astype(jnp.bfloat16)
    new_gate = joint[:, :hidden_units]
    new_up = joint[:, hidden_units:]
    grad_part = lax.dot_general(
        grad_gate_up, stacked, across_last, preferred_element_type=jnp.float32
    ).astype(jnp.bfloat16)
    part_back, prob_back = (
        lax.all_to_all(
            grad_part.reshape(experts, capacity, width_dev),
            "ep",
            split_axis=0,
            concat_axis=0,
            tiled=True,
        ),
        lax.all_to_all(
            grad_prob.reshape(experts, capacity), "ep", split_axis=0, concat_axis=0, tiled=True
        ),
    )
    returned = jnp.take(part_back.reshape(slot_count, width_dev), slot_of, axis=0)
    grad_tokens = jnp.sum(
        returned.reshape(tok_dev, top_count, width_dev).astype(jnp.float32), axis=1
    ).astype(jnp.bfloat16)
    grad_probs = jnp.take(prob_back.reshape(slot_count), slot_of, axis=0).reshape(
        tok_dev, top_count
    )
    return (grad_tokens, grad_probs, new_gate[None], new_up[None], new_down[None])


def solution(mesh):
    return jax.shard_map(
        per_device,
        mesh=mesh,
        in_specs=(
            P("ep", "fs"),
            P("ep", "fs"),
            P("ep", None),
            P("ep", None),
            P("ep", "fs", None),
            P("ep", "fs", None),
            P("ep", None, "fs"),
        ),
        out_specs=(
            P("ep", "fs"),
            P("ep", None),
            P("ep", "fs", None),
            P("ep", "fs", None),
            P("ep", None, "fs"),
        ),
        check_vma=False,
    )
```
